512 devices in a mesh: head: 8 (over x, core), ctx: 64 (over y, z).
Axes of the slice: x: 4, y: 4, z: 16, core: 2. Of those that a mesh axis runs over, the one named last changes fastest.
Arguments:
- queries: bfloat16 [65536, 2048], P('ctx', 'head'), may hold values from -6 to 6
- key_vectors: bfloat16 [65536, 2048], P('ctx', 'head'), may hold values from -6 to 6
- value_vectors: bfloat16 [65536, 2048], P('ctx', 'head'), may hold values from -6 to 6
- out_grad: bfloat16 [65536, 2048], P('ctx', 'head'), may hold values from -6 to 6
- segment_ids: int32 [65536], P('ctx'), may hold values from 0 to 31, never falling along the last dimension, each value on 1 to 16384 neighbouring positions
- head_gain: float32 [16], P('head'), may hold values from 0.3 to 3
Outputs:
- attended: bfloat16 [65536, 2048], P('ctx', 'head')
- grad_queries: bfloat16 [65536, 2048], P('ctx', 'head')
- grad_keys: bfloat16 [65536, 2048], P('ctx', 'head')
- grad_values: bfloat16 [65536, 2048], P('ctx', 'head')
The draws below stay inside these ranges and needn't reach their ends.
Inputs may be any that keep to these rules, and one draw needn't show every extreme that they name: `segment_ids`: document numbers never fall along the sequence; every document covers 1 to 16384 positions and one covers exactly 16384.
All inputs are finite; a program needn't handle non-finite values.
Results may differ from the reference program's by a relative error of at most 0.0058.
Values sent between devices are 32-bit elements; how exact they have to be, the bound alone decides.
No kernel may reach another device: no remote copies, remote signals or barrier semaphores. Data moves between devices by JAX's collectives and lax.ppermute only.
A program may use at most 64 MiB of HBM per device.

```python
import math
import jax
import jax.numpy as jnp
import numpy as np
from jax import lax

HEADS = 16
HS = 128
TOK_DEV = 1024
TOKENS = 65536
DOCS = 32
N_CTX = 64


def levels(rng, extent, shards, least, high):
    level = 1.0
    for dim, parts in shards:
        steps = jax.random.uniform(jax.random.fold_in(jax.random.fold_in(rng, 6), dim), (parts,), jnp.float32, least / len(shards), high / len(shards))
        level = level * jnp.repeat(jnp.exp(steps), extent[dim] // parts).reshape((-1,) + (1,) * (len(extent) - 1 - dim))
    return level


def length_profile(count, total, reach, skew):
    weights = [(1 << 20) // math.isqrt(standing ** skew) + 1 for standing in range(2, count + 1)]
    surplus, holding = total - reach - (count - 1), [1] * (count - 1)
    while surplus > 0:
        movable = [i for i in range(count - 1) if holding[i] < reach]
        pool, remaining = sum([weights[i] for i in movable]), surplus
        for i in movable:
            more = min(reach - holding[i], max(1, remaining * weights[i] // pool), surplus)
            holding[i] = holding[i] + more
            surplus = surplus - more
    return np.array([reach] + holding)


def uneven(stream_key, count, total, most, lean):
    if count == 2:
        one = jax.random.randint(stream_key, (), max(1, total - most), min(most, total - 1) + 1)
        return jnp.stack([one, total - one])
    tallies = jnp.asarray(length_profile(count, total, most, lean), jnp.int32)
    twos = (count - 1) // 2
    donor, taker = tallies[1:1 + 2 * twos:2], tallies[2:2 + 2 * twos:2]
    slack = jnp.minimum(donor - 1, most - taker)
    passed = jax.random.randint(jax.random.fold_in(stream_key, 1), (twos,), 0, 1 << 20) % (slack + 1)
    tallies = tallies.at[1:1 + 2 * twos:2].set(donor - passed).at[2:2 + 2 * twos:2].set(taker + passed)
    return tallies[jax.random.permutation(jax.random.fold_in(stream_key, 2), count)]


def noise(own_key, extent, deviation, most, split=(), dtype=jnp.bfloat16):
    values = deviation * jax.random.normal(own_key, extent, jnp.float32)
    if split:
        values = values * levels(own_key, extent, split, -0.22, 0.18)
    return jnp.clip(values, -most, most).astype(dtype)


def setup_inputs(seed: int = 0) -> dict:
    streams_of = jax.random.split(jax.random.key(seed), 7)
    queries = noise(streams_of[0], (TOKENS, HEADS * HS), 1.0, 6.0, ((0, 64), (1, 8)))
    key_vectors = noise(streams_of[1], (TOKENS, HEADS * HS), 1.0, 6.0, ((0, 64), (1, 8)))
    value_vectors = noise(streams_of[2], (TOKENS, HEADS * HS), 1.0, 6.0, ((0, 64), (1, 8)))
    out_grad = noise(streams_of[3], (TOKENS, HEADS * HS), 1.0, 6.0, ((0, 64), (1, 8)))
    segment_ids = jnp.searchsorted(jnp.cumsum(uneven(streams_of[4], DOCS, TOKENS, TOKENS // 4, 2)), jnp.arange(TOKENS), side="right").astype(jnp.int32)
    head_gain = jnp.clip(jnp.exp(math.log(3.0) - 2.3025851 * jax.random.uniform(streams_of[5], (HEADS,), jnp.float32) ** levels(streams_of[5], (HEADS,), ((0, 8),), -0.2, 0.2)), 0.3, 3.0)
    return {"queries": queries, "key_vectors": key_vectors, "value_vectors": value_vectors, "out_grad": out_grad, "segment_ids": segment_ids, "head_gain": head_gain}


EPS = 1e-05

def allowed_pairs(segments):
    position = jnp.arange(segments.shape[0])
    return (position[:, None] >= position[None, :]) & (segments[:, None] == segments[None, :])

def reference(queries, key_vectors, value_vectors, out_grad, segment_ids, head_gain):
    width = HEADS * HS

    def blocks(array):
        return array.reshape(N_CTX, TOK_DEV, HEADS, HS)
    query_blocks = blocks(queries)
    key_blocks = blocks(key_vectors)
    value_blocks = blocks(value_vectors)
    grad_blocks = blocks(out_grad)
    segment_blocks = segment_ids.reshape(N_CTX, TOK_DEV)
    gain = head_gain.astype(jnp.float32)[None, :, None]
    blank = jnp.zeros((HEADS, HS, HS), jnp.float32)
    start_id = jnp.array(-1, jnp.int32)

    def forward(carry, item):
        prev_close, running = carry
        query_rows, key_rows, value_rows, grad_rows, segments = item
        query_f = query_rows.astype(jnp.float32)
        key_f = key_rows.astype(jnp.float32)
        value_f = value_rows.astype(jnp.float32)
        opening_id = segments[0]
        closing_id = segments[-1]
        allowed = allowed_pairs(segments)[None]
        scores = jnp.einsum('thd,shd->hts', query_f, key_f)
        probs = jnp.where(allowed, scores, 0.0).astype(jnp.bfloat16)
        state_in = jnp.where(prev_close == opening_id, running, 0.0).astype(jnp.bfloat16)
        state_f = state_in.astype(jnp.float32)
        at_open = (segments == opening_id)[:, None, None]
        at_close = (segments == closing_id)[:, None, None]
        attn = jnp.einsum('hts,shd->thd', probs.astype(jnp.float32), value_f)
        attn = attn + jnp.where(at_open, jnp.einsum('thd,hde->the', query_f, state_f), 0.0)
        scaled = attn * gain
        grad_f = grad_rows.astype(jnp.float32)
        power = lax.optimization_barrier(jnp.sum(scaled * scaled, axis=(1, 2)))[:, None, None]
        cross = lax.optimization_barrier(jnp.sum(grad_f * scaled, axis=(1, 2)))[:, None, None]
        scale = lax.rsqrt(power / width + EPS)
        attended = (scaled * scale).astype(jnp.bfloat16)
        inner = (gain * (grad_f * scale - scaled * cross * scale * scale * scale / width)).astype(jnp.bfloat16)
        inner_f = inner.astype(jnp.float32)
        dscores = jnp.einsum('the,she->hts', inner_f, value_f)
        dprobs = jnp.where(allowed, dscores, 0.0).astype(jnp.bfloat16)
        grad_q = jnp.einsum('hts,shd->thd', dprobs.astype(jnp.float32), key_f)
        grad_q = grad_q + jnp.where(at_open, jnp.einsum('the,hde->thd', inner_f, state_f), 0.0)
        tail = jnp.einsum('shd,she->hde', jnp.where(at_close, key_f, 0.0), value_f)
        joined = (prev_close == opening_id) & (opening_id == closing_id)
        running = jnp.where(joined, running + tail, tail)
        back_tail = jnp.einsum('thd,the->hde', jnp.where(at_open, query_f, 0.0), inner_f)
        return ((closing_id, running), (attended, grad_q.astype(jnp.bfloat16), inner, back_tail))
    _, (attended, grad_q, inner, back_tails) = lax.scan(forward, (start_id, blank), (query_blocks, key_blocks, value_blocks, grad_blocks, segment_blocks))

    def backward(carry, item):
        next_open, running = carry
        query_rows, key_rows, value_rows, inner_rows, segments, back_tail = item
        query_f = query_rows.astype(jnp.float32)
        key_f = key_rows.astype(jnp.float32)
        value_f = value_rows.astype(jnp.float32)
        inner_f = inner_rows.astype(jnp.float32)
        opening_id = segments[0]
        closing_id = segments[-1]
        allowed = allowed_pairs(segments)[None]
        scores = jnp.einsum('thd,shd->hts', query_f, key_f)
        probs = jnp.where(allowed, scores, 0.0).astype(jnp.bfloat16).astype(jnp.float32)
        dscores = jnp.einsum('the,she->hts', inner_f, value_f)
        dprobs = jnp.where(allowed, dscores, 0.0).astype(jnp.bfloat16).astype(jnp.float32)
        state_grad = jnp.where(next_open == closing_id, running, 0.0).astype(jnp.bfloat16).astype(jnp.float32)
        at_close = (segments == closing_id)[:, None, None]
        grad_k = jnp.einsum('hts,thd->shd', dprobs, query_f)
        grad_k = grad_k + jnp.where(at_close, jnp.einsum('hde,she->shd', state_grad, value_f), 0.0)
        grad_v = jnp.einsum('hts,the->she', probs, inner_f)
        grad_v = grad_v + jnp.where(at_close, jnp.einsum('hde,shd->she', state_grad, key_f), 0.0)
        joined = (next_open == closing_id) & (opening_id == closing_id)
        running = jnp.where(joined, running + back_tail, back_tail)
        return ((opening_id, running), (grad_k.astype(jnp.bfloat16), grad_v.astype(jnp.bfloat16)))
    _, (grad_k, grad_v) = lax.scan(backward, (start_id, blank), (query_blocks, key_blocks, value_blocks, inner, segment_blocks, back_tails), reverse=True)

    def whole(array):
        return array.reshape(TOKENS, HEADS * HS)
    return (whole(attended), whole(grad_q), whole(grad_k), whole(grad_v))
```

```python
import jax
import jax.numpy as jnp
from jax import lax
from jax.experimental import pallas as pl
from jax.experimental.pallas import tpu as pltpu
from jax.sharding import PartitionSpec as P

HEADS = 16
HS = 128
EPS = 1e-05

ROWS = 1024
LOCAL = 2
N_CTX = 64
STEP = 256
TILES = ROWS // STEP
CHUNK = LOCAL * HS // N_CTX

VMEM = pl.BlockSpec(memory_space=pltpu.VMEM)
SMEM = pl.BlockSpec(memory_space=pltpu.SMEM)
F32 = jnp.float32
BF16 = jnp.bfloat16


def dot(a, b, over, precision=None):
    return lax.dot_general(
        a, b, (((over[0],), (over[1],)), ((), ())), precision=precision, preferred_element_type=F32
    )


def call(kernel, name, outs, gain_last=False):
    def run(*args):
        specs = [VMEM] * (len(args) - 1) + [SMEM if gain_last else VMEM]
        return pl.pallas_call(
            kernel,
            name=name,
            out_shape=[jax.ShapeDtypeStruct(shape, dtype) for shape, dtype in outs],
            in_specs=specs,
            out_specs=[VMEM] * len(outs),
            compiler_params=pltpu.CompilerParams(vmem_limit_bytes=48 << 20),
        )(*args)

    return run


def marks_of(seg_ref):
    seg = seg_ref[...].astype(F32)
    opening, closing = jnp.min(seg), jnp.max(seg)
    n_open = jnp.sum(jnp.where(seg == opening, 1.0, 0.0)).astype(jnp.int32)
    n_close = jnp.sum(jnp.where(seg == closing, 1.0, 0.0)).astype(jnp.int32)
    return opening, closing, n_open, ROWS - n_close


def head_of(ref, h, start=0, size=ROWS):
    return ref[start : start + size, h * HS : (h + 1) * HS]


def positions(start, size):
    return start + lax.broadcasted_iota(jnp.int32, (size, HS), 0)


def put_state(out_ref, states, stride):
    flat = jnp.concatenate(states, axis=0)
    for r in range(CHUNK):
        out_ref[pl.ds(r, N_CTX, stride=stride), :] = flat[r * N_CTX : (r + 1) * N_CTX]


def get_state(ref):
    flat = jnp.concatenate([ref[pl.ds(r, N_CTX, stride=CHUNK), :] for r in range(CHUNK)], axis=0)
    return [flat[h * HS : (h + 1) * HS].astype(BF16) for h in range(LOCAL)]


def tail_kernel(k_ref, v_ref, seg_ref, out_ref):
    opening, closing, _, start = marks_of(seg_ref)
    at_close = positions(0, ROWS) >= start
    tails = []
    for h in range(LOCAL):
        keys = jnp.where(at_close, head_of(k_ref, h).astype(F32), 0.0).astype(BF16)
        tails.append(dot(keys, head_of(v_ref, h), (0, 0)))
    put_state(out_ref, tails, CHUNK + 1)
    lane = lax.broadcasted_iota(jnp.int32, (N_CTX, HS), 1)
    out_ref[pl.ds(CHUNK, N_CTX, stride=CHUNK + 1), :] = jnp.where(lane == 0, opening, closing)


def summed(x_ref, stride, chosen, out_ref):
    x = jnp.concatenate([x_ref[pl.ds(r, N_CTX, stride=stride), :] for r in range(CHUNK)], axis=1)
    y = dot(jnp.where(chosen, 1.0, 0.0), x, (1, 0), lax.Precision.HIGHEST)
    for r in range(CHUNK):
        out_ref[pl.ds(r, N_CTX, stride=CHUNK), :] = y[:, r * HS : (r + 1) * HS]


def square_iota():
    shape = (N_CTX, N_CTX)
    return lax.broadcasted_iota(jnp.int32, shape, 0), lax.broadcasted_iota(jnp.int32, shape, 1)


def as_row(column):
    down, along = square_iota()
    return jnp.sum(jnp.where(down == along, column, 0.0), axis=0, keepdims=True)


def before_kernel(x_ref, out_ref, marks_ref):
    marks = x_ref[pl.ds(CHUNK, N_CTX, stride=CHUNK + 1), :]
    marks_ref[...] = marks
    down, along = square_iota()
    chosen = (along < down) & (as_row(marks[:, 1:2]) == marks[:, 0:1])
    summed(x_ref, CHUNK + 1, chosen, out_ref)


def after_kernel(x_ref, marks_ref, out_ref):
    marks = marks_ref[...]
    down, along = square_iota()
    chosen = (along > down) & (as_row(marks[:, 0:1]) == marks[:, 1:2])
    summed(x_ref, CHUNK, chosen, out_ref)


def column_of(row):
    return jnp.transpose(jnp.broadcast_to(row, (HS, row.shape[1])))


def allowed_tile(seg_ref, i):
    reach = (i + 1) * STEP
    own = column_of(seg_ref[:, i * STEP : reach].astype(F32))
    same = jnp.concatenate([own] * (reach // HS), axis=1) == seg_ref[:, :reach].astype(F32)
    at = i * STEP + lax.broadcasted_iota(jnp.int32, (STEP, reach), 0)
    return same & (lax.broadcasted_iota(jnp.int32, (STEP, reach), 1) <= at)


def local_kernel(q_ref, k_ref, v_ref, row_ref, out_ref):
    for i in range(TILES):
        at, reach = i * STEP, (i + 1) * STEP
        allowed = allowed_tile(row_ref, i)
        for h in range(LOCAL):
            scores = dot(head_of(q_ref, h, at, STEP), head_of(k_ref, h, 0, reach), (1, 1))
            probs = jnp.where(allowed, scores, 0.0).astype(BF16)
            out_ref[at:reach, h * HS : (h + 1) * HS] = dot(
                probs, head_of(v_ref, h, 0, reach), (1, 0)
            )


def attend_kernel(local_ref, q_ref, g_ref, state_ref, seg_ref, gain_ref, scaled_ref, sums_ref):
    _, _, n_open, _ = marks_of(seg_ref)
    states = get_state(state_ref)
    ones = jnp.ones((8, HS), F32)
    for i in range(TILES):
        at, reach = i * STEP, (i + 1) * STEP
        at_open = positions(at, STEP) < n_open
        power = jnp.zeros((STEP, HS), F32)
        cross = jnp.zeros((STEP, HS), F32)
        for h in range(LOCAL):
            carried = dot(head_of(q_ref, h, at, STEP), states[h], (1, 0))
            attn = head_of(local_ref, h, at, STEP) + jnp.where(at_open, carried, 0.0)
            scaled = attn * gain_ref[h]
            scaled_ref[at:reach, h * HS : (h + 1) * HS] = scaled
            power = power + scaled * scaled
            cross = cross + scaled * head_of(g_ref, h, at, STEP).astype(F32)
        sums_ref[0:1, at:reach] = dot(ones, power, (1, 1), lax.Precision.HIGHEST)[0:1]
        sums_ref[1:2, at:reach] = dot(ones, cross, (1, 1), lax.Precision.HIGHEST)[0:1]


def inner_kernel(scaled_ref, g_ref, q_ref, sums_ref, seg_ref, gain_ref, attended_ref, inner_ref, tail_ref):
    _, _, n_open, _ = marks_of(seg_ref)
    width = HEADS * HS
    tails = [jnp.zeros((HS, HS), F32) for _ in range(LOCAL)]
    for i in range(TILES):
        at, reach = i * STEP, (i + 1) * STEP
        scale_row = lax.rsqrt(sums_ref[0:1, at:reach] / width + EPS)
        pull_row = sums_ref[1:2, at:reach] * scale_row * scale_row * scale_row / width
        scale, pull = column_of(scale_row), column_of(pull_row)
        at_open = positions(at, STEP) < n_open
        for h in range(LOCAL):
            cols = slice(h * HS, (h + 1) * HS)
            scaled = scaled_ref[at:reach, cols]
            attended_ref[at:reach, cols] = (scaled * scale).astype(BF16)
            grad = g_ref[at:reach, cols].astype(F32)
            inner = (gain_ref[h] * (grad * scale - scaled * pull)).astype(BF16)
            inner_ref[at:reach, cols] = inner
            query = jnp.where(at_open, q_ref[at:reach, cols].astype(F32), 0.0).astype(BF16)
            tails[h] = tails[h] + dot(query, inner, (0, 0))
    put_state(tail_ref, tails, CHUNK)


def near_queries_kernel(q_ref, k_ref, v_ref, inner_ref, state_ref, seg_ref, row_ref, gq_ref, keys_ref):
    _, _, n_open, _ = marks_of(seg_ref)
    states = get_state(state_ref)
    keys_ref[...] = jnp.zeros(keys_ref.shape, F32)
    for i in range(TILES):
        at, reach = i * STEP, (i + 1) * STEP
        allowed = allowed_tile(row_ref, i)
        at_open = positions(at, STEP) < n_open
        for h in range(LOCAL):
            cols = slice(h * HS, (h + 1) * HS)
            inner = inner_ref[at:reach, cols]
            dscores = dot(inner, v_ref[:reach, cols], (1, 1))
            dprobs = jnp.where(allowed, dscores, 0.0).astype(BF16)
            grad_q = dot(dprobs, k_ref[:reach, cols], (1, 0))
            grad_q = grad_q + jnp.where(at_open, dot(inner, states[h], (1, 1)), 0.0)
            gq_ref[at:reach, cols] = grad_q.astype(BF16)
            keys_ref[:reach, cols] += dot(dprobs, q_ref[at:reach, cols], (0, 0))


def near_values_kernel(q_ref, k_ref, inner_ref, row_ref, values_ref):
    values_ref[...] = jnp.zeros(values_ref.shape, F32)
    for i in range(TILES):
        at, reach = i * STEP, (i + 1) * STEP
        allowed = allowed_tile(row_ref, i)
        for h in range(LOCAL):
            cols = slice(h * HS, (h + 1) * HS)
            scores = dot(q_ref[at:reach, cols], k_ref[:reach, cols], (1, 1))
            probs = jnp.where(allowed, scores, 0.0).astype(BF16)
            values_ref[:reach, cols] += dot(probs, inner_ref[at:reach, cols], (0, 0))


def far_kernel(k_ref, v_ref, keys_ref, values_ref, back_ref, seg_ref, gk_ref, gv_ref):
    _, _, _, start = marks_of(seg_ref)
    backs = get_state(back_ref)
    at_close = positions(0, ROWS) >= start
    for h in range(LOCAL):
        cols = slice(h * HS, (h + 1) * HS)
        far = jnp.where(at_close, dot(v_ref[:, cols], backs[h], (1, 1)), 0.0)
        gk_ref[:, cols] = (keys_ref[:, cols] + far).astype(BF16)
        far = jnp.where(at_close, dot(k_ref[:, cols], backs[h], (1, 0)), 0.0)
        gv_ref[:, cols] = (values_ref[:, cols] + far).astype(BF16)


def exchange(x):
    parts = x.reshape(N_CTX, 1, -1)
    return lax.all_to_all(parts, "ctx", 0, 0, tiled=True).reshape(x.shape)


def over_heads(x):
    pairs = [[2 * i, 2 * i + 1] for i in range(4)]
    rings = [[c + 2 * i for i in range(4)] for c in range(2)]
    x = lax.psum(x, "head", axis_index_groups=pairs)
    return lax.psum(x, "head", axis_index_groups=rings)


def per_device(queries, key_vectors, value_vectors, out_grad, segment_ids, head_gain):
    q, k, v, g, gain = queries, key_vectors, value_vectors, out_grad, head_gain
    seg = segment_ids.reshape(8, HS)
    row = segment_ids.reshape(1, ROWS)
    states = ((N_CTX * CHUNK, HS), F32)
    wide, wide_half = ((ROWS, LOCAL * HS), F32), ((ROWS, LOCAL * HS), BF16)
    payload = ((N_CTX * (CHUNK + 1), HS), F32)

    (tail,) = call(tail_kernel, "tail", [payload])(k, v, seg)
    tails = exchange(tail)
    (local,) = call(local_kernel, "local", [wide])(q, k, v, row)
    before, marks = call(before_kernel, "before", [states, ((N_CTX, HS), F32)])(tails)
    state_in = exchange(before)
    scaled, sums = call(attend_kernel, "attend", [wide, ((2, ROWS), F32)], True)(
        local, q, g, state_in, seg, gain
    )
    sums = over_heads(sums)
    attended, inner, back_tail = call(inner_kernel, "inner", [wide_half, wide_half, states], True)(
        scaled, g, q, sums, seg, gain
    )
    back_tails = exchange(back_tail)
    grad_q, near_k = call(near_queries_kernel, "near_queries", [wide_half, wide])(
        q, k, v, inner, state_in, seg, row
    )
    (after,) = call(after_kernel, "after", [states])(back_tails, marks)
    state_grad = exchange(after)
    (near_v,) = call(near_values_kernel, "near_values", [wide])(q, k, inner, row)
    grad_k, grad_v = call(far_kernel, "far", [wide_half, wide_half])(
        k, v, near_k, near_v, state_grad, seg
    )
    return attended, grad_q, grad_k, grad_v


def solution(mesh):
    both = P("ctx", "head")
    return jax.shard_map(
        per_device,
        mesh=mesh,
        in_specs=(both, both, both, both, P("ctx"), P("head")),
        out_specs=(both, both, both, both),
        check_vma=False,
    )
```

```python
import jax
import jax.numpy as jnp
from jax import lax
from jax.experimental import pallas as pl
from jax.experimental.pallas import tpu as pltpu
from jax.sharding import PartitionSpec as P

HEADS = 16
HS = 128
EPS = 1e-05

ROWS = 1024
LOCAL = 2
N_CTX = 64
STEP = 256
TILES = ROWS // STEP
CHUNK = LOCAL * HS // N_CTX

PEERS = 8
LINES = ROWS // HS

VMEM = pl.BlockSpec(memory_space=pltpu.VMEM)
SMEM = pl.BlockSpec(memory_space=pltpu.SMEM)
HBM = pl.BlockSpec(memory_space=pltpu.HBM)
F32 = jnp.float32
BF16 = jnp.bfloat16


def dot(a, b, over):
    return lax.dot_general(
        a, b, (((over[0],), (over[1],)), ((), ())), preferred_element_type=F32
    )


def thirds(x):
    high = x.astype(BF16)
    rest = x - high.astype(F32)
    middle = rest.astype(BF16)
    return [high, middle, (rest - middle.astype(F32)).astype(BF16)]


def together(pairs, sems):
    copies = [pltpu.make_async_copy(a, b, sems.at[i]) for i, (a, b) in enumerate(pairs)]
    for copy in copies:
        copy.start()
    for copy in copies:
        copy.wait()


def staged(kernel, n_in, n_mid, n_out):
    def run(*refs):
        given, rest = refs[:n_in], list(refs[n_in:])
        sems = rest.pop()
        given_held, out_held = rest[n_mid + n_out :][:n_in], rest[n_mid + n_out :][n_in:]
        middle, out = rest[:n_mid], rest[n_mid : n_mid + n_out]
        together(zip(given, given_held), sems)
        kernel(*given_held, *middle, *out_held)
        together(zip(out_held, out), sems)

    return run


def call(kernel, name, outs, far=(), near=(), specs=None, out_far=0, scratch=(), stage=True):
    far = [pltpu.with_memory_space_constraint(x, pltpu.HBM) for x in far]
    if stage and (far or out_far):
        held_outs = outs[len(outs) - out_far :]
        kernel = staged(kernel, len(far), len(near) + len(outs) - out_far, out_far)
        scratch = [pltpu.VMEM(x.shape, x.dtype) for x in far]
        scratch += [pltpu.VMEM(*held) for held in held_outs]
        scratch += [pltpu.SemaphoreType.DMA((len(far) + out_far,))]
    return pl.pallas_call(
        kernel,
        name=name,
        out_shape=[jax.ShapeDtypeStruct(shape, dtype) for shape, dtype in outs],
        in_specs=[HBM] * len(far) + (specs or [VMEM] * len(near)),
        out_specs=[VMEM] * (len(outs) - out_far) + [HBM] * out_far,
        scratch_shapes=list(scratch),
        compiler_params=pltpu.CompilerParams(vmem_limit_bytes=16 << 20),
    )(*far, *near)


def marks_of(seg_ref):
    seg = seg_ref[...].astype(F32)
    opening, closing = jnp.min(seg), jnp.max(seg)
    n_open = jnp.sum(jnp.where(seg == opening, 1.0, 0.0)).astype(jnp.int32)
    n_close = jnp.sum(jnp.where(seg == closing, 1.0, 0.0)).astype(jnp.int32)
    return opening, closing, n_open, ROWS - n_close


def head_of(ref, h, start=0, size=ROWS):
    return ref[start : start + size, h * HS : (h + 1) * HS]


def positions(start, size):
    return start + lax.broadcasted_iota(jnp.int32, (size, HS), 0)


def put_state(out_ref, states, stride):
    flat = jnp.concatenate(states, axis=0)
    for r in range(CHUNK):
        out_ref[pl.ds(r, N_CTX, stride=stride), :] = flat[r * N_CTX : (r + 1) * N_CTX]


def get_state(ref):
    flat = jnp.concatenate([ref[pl.ds(r, N_CTX, stride=CHUNK), :] for r in range(CHUNK)], axis=0)
    return [flat[h * HS : (h + 1) * HS].astype(BF16) for h in range(LOCAL)]


def tail_kernel(seg_hbm, k_hbm, v_hbm, out_ref, seg_ref, k_ref, v_ref, sems, seg_sem):
    def copies(i):
        rows = pl.ds(i * STEP, STEP)
        return [
            pltpu.make_async_copy(k_hbm.at[rows], k_ref.at[rows], sems.at[0, i]),
            pltpu.make_async_copy(v_hbm.at[rows], v_ref.at[rows], sems.at[1, i]),
        ]

    seg_copy = pltpu.make_async_copy(seg_hbm, seg_ref, seg_sem)
    seg_copy.start()
    for i in range(TILES):
        for copy in copies(i):
            copy.start()
    seg_copy.wait()
    opening, closing, _, start = marks_of(seg_ref)
    lane = lax.broadcasted_iota(jnp.int32, (N_CTX, HS), 1)
    out_ref[pl.ds(CHUNK, N_CTX, stride=CHUNK + 1), :] = jnp.where(lane == 0, opening, closing)
    tails = [jnp.zeros((HS, HS), F32) for _ in range(LOCAL)]
    for i in range(TILES):
        for copy in copies(i):
            copy.wait()
        at_close = positions(i * STEP, STEP) >= start
        for h in range(LOCAL):
            keys = head_of(k_ref, h, i * STEP, STEP).astype(F32)
            keys = jnp.where(at_close, keys, 0.0).astype(BF16)
            tails[h] = tails[h] + dot(keys, head_of(v_ref, h, i * STEP, STEP), (0, 0))
    put_state(out_ref, tails, CHUNK + 1)


def summed(x_ref, stride, chosen, out_ref):
    x = jnp.concatenate([x_ref[pl.ds(r, N_CTX, stride=stride), :] for r in range(CHUNK)], axis=1)
    chosen = jnp.where(chosen, 1.0, 0.0).astype(BF16)
    y = dot(jnp.concatenate([chosen] * 3, axis=1), jnp.concatenate(thirds(x), axis=0), (1, 0))
    for r in range(CHUNK):
        out_ref[pl.ds(r, N_CTX, stride=CHUNK), :] = y[:, r * HS : (r + 1) * HS]


def square_iota():
    shape = (N_CTX, N_CTX)
    return lax.broadcasted_iota(jnp.int32, shape, 0), lax.broadcasted_iota(jnp.int32, shape, 1)


def as_row(column):
    down, along = square_iota()
    return jnp.sum(jnp.where(down == along, column, 0.0), axis=0, keepdims=True)


def before_kernel(x_ref, out_ref, marks_ref):
    marks = x_ref[pl.ds(CHUNK, N_CTX, stride=CHUNK + 1), :]
    marks_ref[...] = marks
    down, along = square_iota()
    chosen = (along < down) & (as_row(marks[:, 1:2]) == marks[:, 0:1])
    summed(x_ref, CHUNK + 1, chosen, out_ref)


def after_kernel(x_ref, marks_ref, out_ref):
    marks = marks_ref[...]
    down, along = square_iota()
    chosen = (along > down) & (as_row(marks[:, 0:1]) == marks[:, 1:2])
    summed(x_ref, CHUNK, chosen, out_ref)


def column_of(row):
    return jnp.transpose(jnp.broadcast_to(row, (HS, row.shape[1])))


def allowed_tile(seg_ref, i):
    reach = (i + 1) * STEP
    own = column_of(seg_ref[:, i * STEP : reach].astype(F32))
    same = jnp.concatenate([own] * (reach // HS), axis=1) == seg_ref[:, :reach].astype(F32)
    at = i * STEP + lax.broadcasted_iota(jnp.int32, (STEP, reach), 0)
    return same & (lax.broadcasted_iota(jnp.int32, (STEP, reach), 1) <= at)


def local_kernel(q_ref, k_ref, v_ref, seg_ref, row_ref, gain_ref, out_ref, open_ref, gains_ref):
    _, _, n_open, _ = marks_of(seg_ref)
    for h in range(LOCAL):
        gains_ref[h : h + 1, :] = jnp.full((1, HS), gain_ref[h], F32)
    for i in range(TILES):
        at, reach = i * STEP, (i + 1) * STEP
        allowed = allowed_tile(row_ref, i)
        at_open = positions(at, STEP) < n_open
        for h in range(LOCAL):
            cols = slice(h * HS, (h + 1) * HS)
            query = q_ref[at:reach, cols]
            scores = dot(query, head_of(k_ref, h, 0, reach), (1, 1))
            probs = jnp.where(allowed, scores, 0.0).astype(BF16)
            out_ref[at:reach, cols] = dot(probs, head_of(v_ref, h, 0, reach), (1, 0))
            open_ref[at:reach, cols] = jnp.where(at_open, query.astype(F32), 0.0).astype(BF16)


def line_of(x):
    ones = jnp.ones((8, 3 * HS), BF16)
    return dot(ones, jnp.concatenate(thirds(x), axis=1), (1, 1))[0:1]


def attend_kernel(g_hbm, local_ref, open_ref, state_ref, gain_ref, scaled_ref, sums_ref, g_ref, sems):
    def copy(i):
        rows = pl.ds(i * STEP, STEP)
        return pltpu.make_async_copy(g_hbm.at[rows], g_ref.at[rows], sems.at[i])

    for i in range(TILES):
        copy(i).start()
    states = get_state(state_ref)
    for i in range(TILES):
        at, reach = i * STEP, (i + 1) * STEP
        power = jnp.zeros((STEP, HS), F32)
        cross = jnp.zeros((STEP, HS), F32)
        copy(i).wait()
        for h in range(LOCAL):
            carried = dot(head_of(open_ref, h, at, STEP), states[h], (1, 0))
            scaled = (head_of(local_ref, h, at, STEP) + carried) * gain_ref[h : h + 1, :]
            scaled_ref[at:reach, h * HS : (h + 1) * HS] = scaled
            power = power + scaled * scaled
            cross = cross + scaled * head_of(g_ref, h, at, STEP).astype(F32)
        for n, line in enumerate((line_of(power), line_of(cross))):
            for j in range(STEP // HS):
                own = line[:, j * HS : (j + 1) * HS]
                first = n * LINES + i * (STEP // HS) + j
                for peer in range(PEERS):
                    sums_ref[peer * 2 * LINES + first : peer * 2 * LINES + first + 1, :] = own


def scale_and_pull(sums_ref):
    lines = 2 * LINES
    total = sums_ref[0:lines]
    for peer in range(1, PEERS):
        total = total + sums_ref[peer * lines : (peer + 1) * lines]
    width = HEADS * HS
    scale = lax.rsqrt(total[:LINES] / width + EPS)
    return scale, total[LINES:] * scale * scale * scale / width


def columns_of(lines, i):
    per = STEP // HS
    return jnp.concatenate([column_of(lines[i * per + j : i * per + j + 1]) for j in range(per)], axis=0)


def inner_kernel(scaled_ref, g_ref, open_ref, sums_ref, gain_ref, inner_ref, tail_ref):
    scale, pull = scale_and_pull(sums_ref)
    tails = [jnp.zeros((HS, HS), F32) for _ in range(LOCAL)]
    for i in range(TILES):
        at, reach = i * STEP, (i + 1) * STEP
        scales, pulls = columns_of(scale, i), columns_of(pull, i)
        for h in range(LOCAL):
            cols = slice(h * HS, (h + 1) * HS)
            grad = g_ref[at:reach, cols].astype(F32)
            inner = (gain_ref[h : h + 1, :] * (grad * scales - scaled_ref[at:reach, cols] * pulls)).astype(BF16)
            inner_ref[at:reach, cols] = inner
            tails[h] = tails[h] + dot(open_ref[at:reach, cols], inner, (0, 0))
    put_state(tail_ref, tails, CHUNK)


def attended_kernel(scaled_ref, sums_ref, out_ref):
    scale, _ = scale_and_pull(sums_ref)
    for i in range(TILES):
        at, reach = i * STEP, (i + 1) * STEP
        scales = columns_of(scale, i)
        for h in range(LOCAL):
            cols = slice(h * HS, (h + 1) * HS)
            out_ref[at:reach, cols] = (scaled_ref[at:reach, cols] * scales).astype(BF16)


def near_queries_kernel(q_ref, k_ref, v_ref, seg_ref, row_ref, inner_ref, state_ref, gq_ref, keys_ref):
    _, _, n_open, _ = marks_of(seg_ref)
    states = get_state(state_ref)
    keys_ref[...] = jnp.zeros(keys_ref.shape, F32)
    for i in range(TILES):
        at, reach = i * STEP, (i + 1) * STEP
        allowed = allowed_tile(row_ref, i)
        at_open = positions(at, STEP) < n_open
        for h in range(LOCAL):
            cols = slice(h * HS, (h + 1) * HS)
            inner = inner_ref[at:reach, cols]
            dscores = dot(inner, v_ref[:reach, cols], (1, 1))
            dprobs = jnp.where(allowed, dscores, 0.0).astype(BF16)
            grad_q = dot(dprobs, k_ref[:reach, cols], (1, 0))
            grad_q = grad_q + jnp.where(at_open, dot(inner, states[h], (1, 1)), 0.0)
            gq_ref[at:reach, cols] = grad_q.astype(BF16)
            keys_ref[:reach, cols] += dot(dprobs, q_ref[at:reach, cols], (0, 0))


def near_values_kernel(q_ref, k_ref, row_ref, inner_ref, values_ref):
    values_ref[...] = jnp.zeros(values_ref.shape, F32)
    for i in range(TILES):
        at, reach = i * STEP, (i + 1) * STEP
        allowed = allowed_tile(row_ref, i)
        for h in range(LOCAL):
            cols = slice(h * HS, (h + 1) * HS)
            scores = dot(q_ref[at:reach, cols], k_ref[:reach, cols], (1, 1))
            probs = jnp.where(allowed, scores, 0.0).astype(BF16)
            values_ref[:reach, cols] += dot(probs, inner_ref[at:reach, cols], (0, 0))


def far_kernel(
    values_hbm, k_ref, v_ref, keys_ref, back_ref, seg_ref, gk_hbm, gv_hbm, values_ref, gk_ref, gv_ref, sems
):
    def copy(n, a, b, i):
        rows = pl.ds(i * STEP, STEP)
        return pltpu.make_async_copy(a.at[rows], b.at[rows], sems.at[n, i])

    for i in range(TILES):
        copy(0, values_hbm, values_ref, i).start()
    _, _, _, start = marks_of(seg_ref)
    backs = get_state(back_ref)
    for i in range(TILES):
        at, reach = i * STEP, (i + 1) * STEP
        at_close = positions(at, STEP) >= start
        for h in range(LOCAL):
            cols = slice(h * HS, (h + 1) * HS)
            far = jnp.where(at_close, dot(v_ref[at:reach, cols], backs[h], (1, 1)), 0.0)
            gk_ref[at:reach, cols] = (keys_ref[at:reach, cols] + far).astype(BF16)
        copy(1, gk_ref, gk_hbm, i).start()
    for i in range(TILES):
        at, reach = i * STEP, (i + 1) * STEP
        at_close = positions(at, STEP) >= start
        copy(0, values_hbm, values_ref, i).wait()
        for h in range(LOCAL):
            cols = slice(h * HS, (h + 1) * HS)
            far = jnp.where(at_close, dot(k_ref[at:reach, cols], backs[h], (1, 0)), 0.0)
            gv_ref[at:reach, cols] = (values_ref[at:reach, cols] + far).astype(BF16)
        copy(2, gv_ref, gv_hbm, i).start()
    for i in range(TILES):
        copy(1, gk_ref, gk_hbm, i).wait()
        copy(2, gv_ref, gv_hbm, i).wait()


def exchange(x):
    parts = x.reshape(N_CTX, 1, -1)
    return lax.all_to_all(parts, "ctx", 0, 0, tiled=True).reshape(x.shape)


def over_heads(x):
    parts = x.reshape(PEERS, 1, -1)
    return lax.all_to_all(parts, "head", 0, 0, tiled=True).reshape(x.shape)


def per_device(queries, key_vectors, value_vectors, out_grad, segment_ids, head_gain):
    q, k, v, g, gain = queries, key_vectors, value_vectors, out_grad, head_gain
    seg = segment_ids.reshape(8, HS)
    row = segment_ids.reshape(1, ROWS)
    states = ((N_CTX * CHUNK, HS), F32)
    wide, wide_half = ((ROWS, LOCAL * HS), F32), ((ROWS, LOCAL * HS), BF16)
    payload = ((N_CTX * (CHUNK + 1), HS), F32)
    sums = ((PEERS * 2 * LINES, HS), F32)
    half_stage = pltpu.VMEM(*wide_half)
    two = [half_stage, half_stage, pltpu.SemaphoreType.DMA((2, TILES))]

    seg_stage, seg_sem = pltpu.VMEM((8, HS), jnp.int32), pltpu.SemaphoreType.DMA
    (tail,) = call(
        tail_kernel, "tail", [payload], (seg, k, v), scratch=[seg_stage, *two, seg_sem], stage=False
    )
    tails = exchange(tail)
    gains = ((LOCAL, HS), F32)
    local, q_open, gains = call(
        local_kernel, "local", [wide, wide_half, gains], (q, k, v, seg, row), (gain,), [SMEM]
    )
    before, marks = call(before_kernel, "before", [states, ((N_CTX, HS), F32)], near=(tails,))
    state_in = exchange(before)
    scaled, part = call(
        attend_kernel,
        "attend",
        [wide, sums],
        (g,),
        (local, q_open, state_in, gains),
        scratch=[half_stage, pltpu.SemaphoreType.DMA((TILES,))],
        stage=False,
    )
    total = over_heads(part)
    inner, back_tail = call(
        inner_kernel, "inner", [wide_half, states], (), (scaled, g, q_open, total, gains)
    )
    back_tails = exchange(back_tail)
    (attended,) = call(attended_kernel, "attended", [wide_half], near=(scaled, total))
    grad_q, near_k = call(
        near_queries_kernel, "near_queries", [wide_half, wide], (q, k, v, seg, row), (inner, state_in)
    )
    (after,) = call(after_kernel, "after", [states], near=(back_tails, marks))
    state_grad = exchange(after)
    (near_v,) = call(near_values_kernel, "near_values", [wide], (q, k, row), (inner,), out_far=1)
    grad_k, grad_v = call(
        far_kernel,
        "far",
        [wide_half, wide_half],
        (near_v,),
        (k, v, near_k, state_grad, seg),
        out_far=2,
        scratch=[pltpu.VMEM(*wide), half_stage, half_stage, pltpu.SemaphoreType.DMA((3, TILES))],
        stage=False,
    )
    return attended, grad_q, grad_k, grad_v


def solution(mesh):
    both = P("ctx", "head")
    return jax.shard_map(
        per_device,
        mesh=mesh,
        in_specs=(both, both, both, both, P("ctx"), P("head")),
        out_specs=(both, both, both, both),
        check_vma=False,
    )
```

```python
import jax
import jax.numpy as jnp
from jax import lax
from jax.experimental import pallas as pl
from jax.experimental.pallas import tpu as pltpu
from jax.sharding import PartitionSpec as P

HEADS = 16
HS = 128
EPS = 1e-05

ROWS = 1024
LOCAL = 2
RING = 16
N_ROWS = 4
STEP = 256
TILES = ROWS // STEP
CHUNK = LOCAL * HS // RING

PEERS = 8
LINES = ROWS // HS

VMEM = pl.BlockSpec(memory_space=pltpu.VMEM)
SMEM = pl.BlockSpec(memory_space=pltpu.SMEM)
HBM = pl.BlockSpec(memory_space=pltpu.HBM)
F32 = jnp.float32
BF16 = jnp.bfloat16


def dot(a, b, over):
    return lax.dot_general(
        a, b, (((over[0],), (over[1],)), ((), ())), preferred_element_type=F32
    )


def thirds(x):
    high = x.astype(BF16)
    rest = x - high.astype(F32)
    middle = rest.astype(BF16)
    return [high, middle, (rest - middle.astype(F32)).astype(BF16)]


def together(pairs, sems):
    copies = [pltpu.make_async_copy(a, b, sems.at[i]) for i, (a, b) in enumerate(pairs)]
    for copy in copies:
        copy.start()
    for copy in copies:
        copy.wait()


def staged(kernel, n_in, n_mid, n_out):
    def run(*refs):
        given, rest = refs[:n_in], list(refs[n_in:])
        sems = rest.pop()
        given_held, out_held = rest[n_mid + n_out :][:n_in], rest[n_mid + n_out :][n_in:]
        middle, out = rest[:n_mid], rest[n_mid : n_mid + n_out]
        together(zip(given, given_held), sems)
        kernel(*given_held, *middle, *out_held)
        together(zip(out_held, out), sems)

    return run


def call(kernel, name, outs, far=(), near=(), specs=None, out_far=0, scratch=(), stage=True):
    far = [pltpu.with_memory_space_constraint(x, pltpu.HBM) for x in far]
    if stage and (far or out_far):
        held_outs = outs[len(outs) - out_far :]
        kernel = staged(kernel, len(far), len(near) + len(outs) - out_far, out_far)
        scratch = [pltpu.VMEM(x.shape, x.dtype) for x in far]
        scratch += [pltpu.VMEM(*held) for held in held_outs]
        scratch += [pltpu.SemaphoreType.DMA((len(far) + out_far,))]
    return pl.pallas_call(
        kernel,
        name=name,
        out_shape=[jax.ShapeDtypeStruct(shape, dtype) for shape, dtype in outs],
        in_specs=[HBM] * len(far) + (specs or [VMEM] * len(near)),
        out_specs=[VMEM] * (len(outs) - out_far) + [HBM] * out_far,
        scratch_shapes=list(scratch),
        compiler_params=pltpu.CompilerParams(vmem_limit_bytes=16 << 20),
    )(*far, *near)


def marks_of(seg_ref):
    seg = seg_ref[...].astype(F32)
    opening, closing = jnp.min(seg), jnp.max(seg)
    n_open = jnp.sum(jnp.where(seg == opening, 1.0, 0.0)).astype(jnp.int32)
    n_close = jnp.sum(jnp.where(seg == closing, 1.0, 0.0)).astype(jnp.int32)
    return opening, closing, n_open, ROWS - n_close


def head_of(ref, h, start=0, size=ROWS):
    return ref[start : start + size, h * HS : (h + 1) * HS]


def positions(start, size):
    return start + lax.broadcasted_iota(jnp.int32, (size, HS), 0)


def put_state(out_ref, states, stride):
    flat = jnp.concatenate(states, axis=0)
    for r in range(CHUNK):
        out_ref[pl.ds(r, RING, stride=stride), :] = flat[r * RING : (r + 1) * RING]


def get_state(ref):
    flat = jnp.concatenate([ref[pl.ds(r, RING, stride=CHUNK), :] for r in range(CHUNK)], axis=0)
    return [flat[h * HS : (h + 1) * HS].astype(BF16) for h in range(LOCAL)]


def tail_kernel(seg_hbm, k_hbm, v_hbm, out_ref, seg_ref, k_ref, v_ref, sems, seg_sem):
    def copies(i):
        rows = pl.ds(i * STEP, STEP)
        return [
            pltpu.make_async_copy(k_hbm.at[rows], k_ref.at[rows], sems.at[0, i]),
            pltpu.make_async_copy(v_hbm.at[rows], v_ref.at[rows], sems.at[1, i]),
        ]

    seg_copy = pltpu.make_async_copy(seg_hbm, seg_ref, seg_sem)
    seg_copy.start()
    for i in range(TILES):
        for copy in copies(i):
            copy.start()
    seg_copy.wait()
    opening, closing, _, start = marks_of(seg_ref)
    lane = lax.broadcasted_iota(jnp.int32, (RING, HS), 1)
    out_ref[pl.ds(CHUNK, RING, stride=CHUNK + 1), :] = jnp.where(lane == 0, opening, closing) + 1.0
    tails = [jnp.zeros((HS, HS), F32) for _ in range(LOCAL)]
    for i in range(TILES):
        for copy in copies(i):
            copy.wait()
        at_close = positions(i * STEP, STEP) >= start
        for h in range(LOCAL):
            keys = head_of(k_ref, h, i * STEP, STEP).astype(F32)
            keys = jnp.where(at_close, keys, 0.0).astype(BF16)
            tails[h] = tails[h] + dot(keys, head_of(v_ref, h, i * STEP, STEP), (0, 0))
    put_state(out_ref, tails, CHUNK + 1)


def chunks_of(x_ref, stride, more=None):
    parts = []
    for r in range(CHUNK):
        part = x_ref[pl.ds(r, RING, stride=stride), :]
        if more is not None:
            part = jnp.concatenate([part, jnp.broadcast_to(more[r : r + 1], (8, HS))], axis=0)
        parts.append(part)
    return jnp.concatenate(parts, axis=1)


def summed(chosen, x, out_ref, stride):
    chosen = jnp.where(chosen, 1.0, 0.0).astype(BF16)
    y = dot(jnp.concatenate([chosen] * 3, axis=1), jnp.concatenate(thirds(x), axis=0), (1, 0))
    for r in range(CHUNK):
        own = y[:, r * HS : (r + 1) * HS]
        if stride:
            out_ref[pl.ds(r, RING, stride=stride), :] = own
        else:
            out_ref[r : r + 1, :] = own[0:1]


def iotas(down, along):
    return [lax.broadcasted_iota(jnp.int32, (down, along), d) for d in range(2)]


def as_row(column):
    n = column.shape[0]
    down, along = iotas(n, n)
    return jnp.sum(jnp.where(down == along, column, 0.0), axis=0, keepdims=True)


def row_end_kernel(x_ref, out_ref, marks_ref):
    marks = x_ref[pl.ds(CHUNK, RING, stride=CHUNK + 1), :]
    marks_ref[...] = marks
    closing = marks[RING - 1 : RING, 1:2]
    chosen = jnp.broadcast_to(as_row(marks[:, 1:2]) == closing, (8, RING))
    summed(chosen, chunks_of(x_ref, CHUNK + 1), out_ref, 0)
    out_ref[CHUNK:, :] = jnp.broadcast_to(closing, (8, HS))


def row_start_kernel(x_ref, marks_ref, out_ref):
    opening = marks_ref[0:1, 0:1]
    chosen = jnp.broadcast_to(as_row(marks_ref[:, 0:1]) == opening, (8, RING))
    summed(chosen, chunks_of(x_ref, CHUNK), out_ref, 0)
    out_ref[CHUNK:, :] = jnp.broadcast_to(opening, (8, HS))


def before_kernel(x_ref, marks_ref, more_ref, out_ref):
    closing = jnp.concatenate([marks_ref[:, 1:2], more_ref[CHUNK:, 0:1]], axis=0)
    down, along = iotas(RING, RING + 8)
    chosen = (as_row(closing) == marks_ref[:, 0:1]) & ((along < down) | (along == RING))
    summed(chosen, chunks_of(x_ref, CHUNK + 1, more_ref[:CHUNK, :]), out_ref, CHUNK)


def after_kernel(x_ref, marks_ref, more_ref, out_ref):
    opening = jnp.concatenate([marks_ref[:, 0:1], more_ref[CHUNK:, 0:1]], axis=0)
    down, along = iotas(RING, RING + 8)
    chosen = (as_row(opening) == marks_ref[:, 1:2]) & (along > down) & (along <= RING)
    summed(chosen, chunks_of(x_ref, CHUNK, more_ref[:CHUNK, :]), out_ref, CHUNK)


def column_of(row):
    return jnp.transpose(jnp.broadcast_to(row, (HS, row.shape[1])))


def allowed_tile(seg_ref, i):
    reach = (i + 1) * STEP
    own = column_of(seg_ref[:, i * STEP : reach].astype(F32))
    same = jnp.concatenate([own] * (reach // HS), axis=1) == seg_ref[:, :reach].astype(F32)
    at = i * STEP + lax.broadcasted_iota(jnp.int32, (STEP, reach), 0)
    return same & (lax.broadcasted_iota(jnp.int32, (STEP, reach), 1) <= at)


def local_kernel(q_ref, k_ref, v_ref, seg_ref, row_ref, gain_ref, out_ref, open_ref, gains_ref):
    _, _, n_open, _ = marks_of(seg_ref)
    for h in range(LOCAL):
        gains_ref[h : h + 1, :] = jnp.full((1, HS), gain_ref[h], F32)
    for i in range(TILES):
        at, reach = i * STEP, (i + 1) * STEP
        allowed = allowed_tile(row_ref, i)
        at_open = positions(at, STEP) < n_open
        for h in range(LOCAL):
            cols = slice(h * HS, (h + 1) * HS)
            query = q_ref[at:reach, cols]
            scores = dot(query, head_of(k_ref, h, 0, reach), (1, 1))
            probs = jnp.where(allowed, scores, 0.0).astype(BF16)
            out_ref[at:reach, cols] = dot(probs, head_of(v_ref, h, 0, reach), (1, 0))
            open_ref[at:reach, cols] = jnp.where(at_open, query.astype(F32), 0.0).astype(BF16)


def line_of(x):
    ones = jnp.ones((8, 3 * HS), BF16)
    return dot(ones, jnp.concatenate(thirds(x), axis=1), (1, 1))[0:1]


def attend_kernel(g_hbm, local_ref, open_ref, state_ref, gain_ref, scaled_ref, sums_ref, g_ref, sems):
    def copy(i):
        rows = pl.ds(i * STEP, STEP)
        return pltpu.make_async_copy(g_hbm.at[rows], g_ref.at[rows], sems.at[i])

    for i in range(TILES):
        copy(i).start()
    states = get_state(state_ref)

    def put(n, i, x):
        line = line_of(x)
        for j in range(STEP // HS):
            first = n * LINES + i * (STEP // HS) + j
            for peer in range(PEERS):
                row = peer * 2 * LINES + first
                sums_ref[row : row + 1, :] = line[:, j * HS : (j + 1) * HS]

    for i in range(TILES):
        at, reach = i * STEP, (i + 1) * STEP
        power = jnp.zeros((STEP, HS), F32)
        for h in range(LOCAL):
            carried = dot(head_of(open_ref, h, at, STEP), states[h], (1, 0))
            scaled = (head_of(local_ref, h, at, STEP) + carried) * gain_ref[h : h + 1, :]
            scaled_ref[at:reach, h * HS : (h + 1) * HS] = scaled
            power = power + scaled * scaled
        put(0, i, power)
    for i in range(TILES):
        copy(i).wait()
        cross = jnp.zeros((STEP, HS), F32)
        for h in range(LOCAL):
            cross = cross + head_of(scaled_ref, h, i * STEP, STEP) * head_of(g_ref, h, i * STEP, STEP).astype(F32)
        put(1, i, cross)


def scale_and_pull(sums_ref):
    lines = 2 * LINES
    total = sums_ref[0:lines]
    for peer in range(1, PEERS):
        total = total + sums_ref[peer * lines : (peer + 1) * lines]
    width = HEADS * HS
    scale = lax.rsqrt(total[:LINES] / width + EPS)
    return scale, total[LINES:] * scale * scale * scale / width


def columns_of(lines, i):
    per = STEP // HS
    return jnp.concatenate([column_of(lines[i * per + j : i * per + j + 1]) for j in range(per)], axis=0)


def inner_kernel(scaled_ref, g_ref, open_ref, sums_ref, gain_ref, inner_ref, tail_ref):
    scale, pull = scale_and_pull(sums_ref)
    tails = [jnp.zeros((HS, HS), F32) for _ in range(LOCAL)]
    for i in range(TILES):
        at, reach = i * STEP, (i + 1) * STEP
        scales, pulls = columns_of(scale, i), columns_of(pull, i)
        for h in range(LOCAL):
            cols = slice(h * HS, (h + 1) * HS)
            grad = g_ref[at:reach, cols].astype(F32)
            inner = (gain_ref[h : h + 1, :] * (grad * scales - scaled_ref[at:reach, cols] * pulls)).astype(BF16)
            inner_ref[at:reach, cols] = inner
            tails[h] = tails[h] + dot(open_ref[at:reach, cols], inner, (0, 0))
    put_state(tail_ref, tails, CHUNK)


def attended_kernel(scaled_ref, sums_ref, out_ref):
    scale, _ = scale_and_pull(sums_ref)
    for i in range(TILES):
        at, reach = i * STEP, (i + 1) * STEP
        scales = columns_of(scale, i)
        for h in range(LOCAL):
            cols = slice(h * HS, (h + 1) * HS)
            out_ref[at:reach, cols] = (scaled_ref[at:reach, cols] * scales).astype(BF16)


def near_queries_kernel(q_ref, k_ref, v_ref, seg_ref, row_ref, inner_ref, state_ref, gq_ref, keys_ref):
    _, _, n_open, _ = marks_of(seg_ref)
    states = get_state(state_ref)
    keys_ref[...] = jnp.zeros(keys_ref.shape, F32)
    for i in range(TILES):
        at, reach = i * STEP, (i + 1) * STEP
        allowed = allowed_tile(row_ref, i)
        at_open = positions(at, STEP) < n_open
        for h in range(LOCAL):
            cols = slice(h * HS, (h + 1) * HS)
            inner = inner_ref[at:reach, cols]
            dscores = dot(inner, v_ref[:reach, cols], (1, 1))
            dprobs = jnp.where(allowed, dscores, 0.0).astype(BF16)
            grad_q = dot(dprobs, k_ref[:reach, cols], (1, 0))
            grad_q = grad_q + jnp.where(at_open, dot(inner, states[h], (1, 1)), 0.0)
            gq_ref[at:reach, cols] = grad_q.astype(BF16)
            keys_ref[:reach, cols] += dot(dprobs, q_ref[at:reach, cols], (0, 0))


def near_values_kernel(q_ref, k_ref, row_ref, inner_ref, values_ref):
    values_ref[...] = jnp.zeros(values_ref.shape, F32)
    for i in range(TILES):
        at, reach = i * STEP, (i + 1) * STEP
        allowed = allowed_tile(row_ref, i)
        for h in range(LOCAL):
            cols = slice(h * HS, (h + 1) * HS)
            scores = dot(q_ref[at:reach, cols], k_ref[:reach, cols], (1, 1))
            probs = jnp.where(allowed, scores, 0.0).astype(BF16)
            values_ref[:reach, cols] += dot(probs, inner_ref[at:reach, cols], (0, 0))


def far_kernel(
    values_hbm, k_ref, v_ref, keys_ref, back_ref, seg_ref, gk_hbm, gv_hbm, values_ref, gk_ref, gv_ref, sems
):
    def copy(n, a, b, i):
        rows = pl.ds(i * STEP, STEP)
        return pltpu.make_async_copy(a.at[rows], b.at[rows], sems.at[n, i])

    for i in range(TILES):
        copy(0, values_hbm, values_ref, i).start()
    _, _, _, start = marks_of(seg_ref)
    backs = get_state(back_ref)
    for i in range(TILES):
        at, reach = i * STEP, (i + 1) * STEP
        at_close = positions(at, STEP) >= start
        for h in range(LOCAL):
            cols = slice(h * HS, (h + 1) * HS)
            far = jnp.where(at_close, dot(v_ref[at:reach, cols], backs[h], (1, 1)), 0.0)
            gk_ref[at:reach, cols] = (keys_ref[at:reach, cols] + far).astype(BF16)
        copy(1, gk_ref, gk_hbm, i).start()
    for i in range(TILES):
        at, reach = i * STEP, (i + 1) * STEP
        at_close = positions(at, STEP) >= start
        copy(0, values_hbm, values_ref, i).wait()
        for h in range(LOCAL):
            cols = slice(h * HS, (h + 1) * HS)
            far = jnp.where(at_close, dot(k_ref[at:reach, cols], backs[h], (1, 0)), 0.0)
            gv_ref[at:reach, cols] = (values_ref[at:reach, cols] + far).astype(BF16)
        copy(2, gv_ref, gv_hbm, i).start()
    for i in range(TILES):
        copy(1, gk_ref, gk_hbm, i).wait()
        copy(2, gv_ref, gv_hbm, i).wait()


def exchange(x):
    parts = x.reshape(RING, 1, -1)
    rings = [[y * RING + z for z in range(RING)] for y in range(N_ROWS)]
    out = lax.all_to_all(parts, "ctx", 0, 0, axis_index_groups=rings, tiled=True)
    return out.reshape(x.shape)


def to_row(x, by):
    pairs = [(i, i + by * RING) for i in range(N_ROWS * RING)]
    return lax.ppermute(x, "ctx", [(a, b) for a, b in pairs if 0 <= b < N_ROWS * RING])


def over_heads(x):
    parts = x.reshape(PEERS, 1, -1)
    return lax.all_to_all(parts, "head", 0, 0, tiled=True).reshape(x.shape)


def per_device(queries, key_vectors, value_vectors, out_grad, segment_ids, head_gain):
    q, k, v, g, gain = queries, key_vectors, value_vectors, out_grad, head_gain
    seg = segment_ids.reshape(8, HS)
    row = segment_ids.reshape(1, ROWS)
    states = ((RING * CHUNK, HS), F32)
    wide, wide_half = ((ROWS, LOCAL * HS), F32), ((ROWS, LOCAL * HS), BF16)
    payload = ((RING * (CHUNK + 1), HS), F32)
    sums = ((PEERS * 2 * LINES, HS), F32)
    half_stage = pltpu.VMEM(*wide_half)
    two = [half_stage, half_stage, pltpu.SemaphoreType.DMA((2, TILES))]

    seg_stage, seg_sem = pltpu.VMEM((8, HS), jnp.int32), pltpu.SemaphoreType.DMA
    (tail,) = call(
        tail_kernel, "tail", [payload], (seg, k, v), scratch=[seg_stage, *two, seg_sem], stage=False
    )
    tails = exchange(tail)
    gains = ((LOCAL, HS), F32)
    local, q_open, gains = call(
        local_kernel, "local", [wide, wide_half, gains], (q, k, v, seg, row), (gain,), [SMEM]
    )
    carry = ((CHUNK + 8, HS), F32)
    row_end, marks = call(row_end_kernel, "row_end", [carry, ((RING, HS), F32)], near=(tails,))
    (before,) = call(before_kernel, "before", [states], near=(tails, marks, to_row(row_end, 1)))
    state_in = exchange(before)
    scaled, part = call(
        attend_kernel,
        "attend",
        [wide, sums],
        (g,),
        (local, q_open, state_in, gains),
        scratch=[half_stage, pltpu.SemaphoreType.DMA((TILES,))],
        stage=False,
    )
    total = over_heads(part)
    inner, back_tail = call(
        inner_kernel, "inner", [wide_half, states], (), (scaled, g, q_open, total, gains)
    )
    back_tails = exchange(back_tail)
    (attended,) = call(attended_kernel, "attended", [wide_half], near=(scaled, total))
    (near_v,) = call(near_values_kernel, "near_values", [wide], (q, k, row), (inner,), out_far=1)
    grad_q, near_k = call(
        near_queries_kernel, "near_queries", [wide_half, wide], (q, k, v, seg, row), (inner, state_in)
    )
    back_tails, near_v, attended = lax.optimization_barrier((back_tails, near_v, attended))
    (row_start,) = call(row_start_kernel, "row_start", [carry], near=(back_tails, marks))
    (after,) = call(after_kernel, "after", [states], near=(back_tails, marks, to_row(row_start, -1)))
    state_grad = exchange(after)
    grad_k, grad_v = call(
        far_kernel,
        "far",
        [wide_half, wide_half],
        (near_v,),
        (k, v, near_k, state_grad, seg),
        out_far=2,
        scratch=[pltpu.VMEM(*wide), half_stage, half_stage, pltpu.SemaphoreType.DMA((3, TILES))],
        stage=False,
    )
    return attended, grad_q, grad_k, grad_v


def solution(mesh):
    both = P("ctx", "head")
    return jax.shard_map(
        per_device,
        mesh=mesh,
        in_specs=(both, both, both, both, P("ctx"), P("head")),
        out_specs=(both, both, both, both),
        check_vma=False,
    )
```

```python
import jax
import jax.numpy as jnp
from jax import lax
from jax.experimental import pallas as pl
from jax.experimental.pallas import tpu as pltpu
from jax.sharding import PartitionSpec as P

HEADS = 16
HS = 128
EPS = 1e-05

ROWS = 1024
LOCAL = 2
RING = 16
N_ROWS = 4
STEP = 256
TILES = ROWS // STEP
CHUNK = LOCAL * HS // RING

PEERS = 8
LINES = ROWS // HS

VMEM = pl.BlockSpec(memory_space=pltpu.VMEM)
SMEM = pl.BlockSpec(memory_space=pltpu.SMEM)
HBM = pl.BlockSpec(memory_space=pltpu.HBM)
F32 = jnp.float32
BF16 = jnp.bfloat16


def dot(a, b, over):
    return lax.dot_general(
        a, b, (((over[0],), (over[1],)), ((), ())), preferred_element_type=F32
    )


def thirds(x):
    high = x.astype(BF16)
    rest = x - high.astype(F32)
    middle = rest.astype(BF16)
    return [high, middle, (rest - middle.astype(F32)).astype(BF16)]


def together(pairs, sems):
    copies = [pltpu.make_async_copy(a, b, sems.at[i]) for i, (a, b) in enumerate(pairs)]
    for copy in copies:
        copy.start()
    for copy in copies:
        copy.wait()


def staged(kernel, n_in, n_mid, n_out):
    def run(*refs):
        given, rest = refs[:n_in], list(refs[n_in:])
        sems = rest.pop()
        given_held, out_held = rest[n_mid + n_out :][:n_in], rest[n_mid + n_out :][n_in:]
        middle, out = rest[:n_mid], rest[n_mid : n_mid + n_out]
        together(zip(given, given_held), sems)
        kernel(*given_held, *middle, *out_held)
        together(zip(out_held, out), sems)

    return run


def call(kernel, name, outs, far=(), near=(), specs=None, out_far=0, scratch=(), stage=True):
    far = [pltpu.with_memory_space_constraint(x, pltpu.HBM) for x in far]
    if stage and (far or out_far):
        held_outs = outs[len(outs) - out_far :]
        kernel = staged(kernel, len(far), len(near) + len(outs) - out_far, out_far)
        scratch = [pltpu.VMEM(x.shape, x.dtype) for x in far]
        scratch += [pltpu.VMEM(*held) for held in held_outs]
        scratch += [pltpu.SemaphoreType.DMA((len(far) + out_far,))]
    return pl.pallas_call(
        kernel,
        name=name,
        out_shape=[jax.ShapeDtypeStruct(shape, dtype) for shape, dtype in outs],
        in_specs=[HBM] * len(far) + (specs or [VMEM] * len(near)),
        out_specs=[VMEM] * (len(outs) - out_far) + [HBM] * out_far,
        scratch_shapes=list(scratch),
        compiler_params=pltpu.CompilerParams(vmem_limit_bytes=16 << 20),
    )(*far, *near)


def marks_of(seg_ref):
    seg = seg_ref[...].astype(F32)
    opening, closing = jnp.min(seg), jnp.max(seg)
    n_open = jnp.sum(jnp.where(seg == opening, 1.0, 0.0)).astype(jnp.int32)
    n_close = jnp.sum(jnp.where(seg == closing, 1.0, 0.0)).astype(jnp.int32)
    return opening, closing, n_open, ROWS - n_close


def head_of(ref, h, start=0, size=ROWS):
    return ref[start : start + size, h * HS : (h + 1) * HS]


def positions(start, size):
    return start + lax.broadcasted_iota(jnp.int32, (size, HS), 0)


def put_state(out_ref, states, stride):
    flat = jnp.concatenate(states, axis=0)
    for r in range(CHUNK):
        out_ref[pl.ds(r, RING, stride=stride), :] = flat[r * RING : (r + 1) * RING]


def get_state(ref):
    flat = jnp.concatenate([ref[pl.ds(r, RING, stride=CHUNK), :] for r in range(CHUNK)], axis=0)
    return [flat[h * HS : (h + 1) * HS].astype(BF16) for h in range(LOCAL)]


TAIL_TILES = 2
TAIL_STEP = ROWS // TAIL_TILES


def tail_kernel(seg_hbm, k_hbm, v_hbm, out_ref, seg_ref, k_ref, v_ref, sems, seg_sem):
    def copies(i):
        rows = pl.ds(i * TAIL_STEP, TAIL_STEP)
        return [
            pltpu.make_async_copy(k_hbm.at[rows], k_ref.at[rows], sems.at[0, i]),
            pltpu.make_async_copy(v_hbm.at[rows], v_ref.at[rows], sems.at[1, i]),
        ]

    seg_copy = pltpu.make_async_copy(seg_hbm, seg_ref, seg_sem)
    seg_copy.start()
    for i in range(TAIL_TILES):
        for copy in copies(i):
            copy.start()
    seg_copy.wait()
    opening, closing, _, start = marks_of(seg_ref)
    lane = lax.broadcasted_iota(jnp.int32, (RING, HS), 1)
    out_ref[pl.ds(CHUNK, RING, stride=CHUNK + 1), :] = jnp.where(lane == 0, opening, closing) + 1.0
    tails = [jnp.zeros((HS, HS), F32) for _ in range(LOCAL)]
    for i in range(TAIL_TILES):
        for copy in copies(i):
            copy.wait()
        at_close = positions(i * TAIL_STEP, TAIL_STEP) >= start
        for h in range(LOCAL):
            keys = head_of(k_ref, h, i * TAIL_STEP, TAIL_STEP).astype(F32)
            keys = jnp.where(at_close, keys, 0.0).astype(BF16)
            tails[h] = tails[h] + dot(keys, head_of(v_ref, h, i * TAIL_STEP, TAIL_STEP), (0, 0))
    put_state(out_ref, tails, CHUNK + 1)


def chunks_of(x_ref, stride, more=None):
    parts = []
    for r in range(CHUNK):
        part = x_ref[pl.ds(r, RING, stride=stride), :]
        if more is not None:
            part = jnp.concatenate([part, jnp.broadcast_to(more[r : r + 1], (8, HS))], axis=0)
        parts.append(part)
    return jnp.concatenate(parts, axis=1)


def summed(chosen, x, out_ref, stride):
    chosen = jnp.where(chosen, 1.0, 0.0).astype(BF16)
    y = dot(jnp.concatenate([chosen] * 3, axis=1), jnp.concatenate(thirds(x), axis=0), (1, 0))
    for r in range(CHUNK):
        own = y[:, r * HS : (r + 1) * HS]
        if stride:
            out_ref[pl.ds(r, RING, stride=stride), :] = own
        else:
            out_ref[r : r + 1, :] = own[0:1]


def iotas(down, along):
    return [lax.broadcasted_iota(jnp.int32, (down, along), d) for d in range(2)]


def as_row(column):
    n = column.shape[0]
    down, along = iotas(n, n)
    return jnp.sum(jnp.where(down == along, column, 0.0), axis=0, keepdims=True)


def row_end_kernel(x_ref, out_ref, marks_ref):
    marks = x_ref[pl.ds(CHUNK, RING, stride=CHUNK + 1), :]
    marks_ref[...] = marks
    closing = marks[RING - 1 : RING, 1:2]
    chosen = jnp.broadcast_to(as_row(marks[:, 1:2]) == closing, (8, RING))
    summed(chosen, chunks_of(x_ref, CHUNK + 1), out_ref, 0)
    out_ref[CHUNK:, :] = jnp.broadcast_to(closing, (8, HS))


def row_start_kernel(x_ref, marks_ref, out_ref):
    opening = marks_ref[0:1, 0:1]
    chosen = jnp.broadcast_to(as_row(marks_ref[:, 0:1]) == opening, (8, RING))
    summed(chosen, chunks_of(x_ref, CHUNK), out_ref, 0)
    out_ref[CHUNK:, :] = jnp.broadcast_to(opening, (8, HS))


def before_kernel(x_ref, marks_ref, more_ref, out_ref):
    closing = jnp.concatenate([marks_ref[:, 1:2], more_ref[CHUNK:, 0:1]], axis=0)
    down, along = iotas(RING, RING + 8)
    chosen = (as_row(closing) == marks_ref[:, 0:1]) & ((along < down) | (along == RING))
    summed(chosen, chunks_of(x_ref, CHUNK + 1, more_ref[:CHUNK, :]), out_ref, CHUNK)


def after_kernel(x_ref, marks_ref, more_ref, out_ref):
    opening = jnp.concatenate([marks_ref[:, 0:1], more_ref[CHUNK:, 0:1]], axis=0)
    down, along = iotas(RING, RING + 8)
    chosen = (as_row(opening) == marks_ref[:, 1:2]) & (along > down) & (along <= RING)
    summed(chosen, chunks_of(x_ref, CHUNK, more_ref[:CHUNK, :]), out_ref, CHUNK)


def column_of(row):
    return jnp.transpose(jnp.broadcast_to(row, (HS, row.shape[1])))


def allowed_tile(seg_ref, i):
    reach = (i + 1) * STEP
    own = column_of(seg_ref[:, i * STEP : reach].astype(F32))
    same = jnp.concatenate([own] * (reach // HS), axis=1) == seg_ref[:, :reach].astype(F32)
    at = i * STEP + lax.broadcasted_iota(jnp.int32, (STEP, reach), 0)
    return same & (lax.broadcasted_iota(jnp.int32, (STEP, reach), 1) <= at)


def local_kernel(q_ref, k_ref, v_ref, seg_ref, row_ref, gain_ref, out_ref, open_ref, gains_ref):
    _, _, n_open, _ = marks_of(seg_ref)
    for h in range(LOCAL):
        gains_ref[h : h + 1, :] = jnp.full((1, HS), gain_ref[h], F32)
    for i in range(TILES):
        at, reach = i * STEP, (i + 1) * STEP
        allowed = allowed_tile(row_ref, i)
        at_open = positions(at, STEP) < n_open
        for h in range(LOCAL):
            cols = slice(h * HS, (h + 1) * HS)
            query = q_ref[at:reach, cols]
            scores = dot(query, head_of(k_ref, h, 0, reach), (1, 1))
            probs = jnp.where(allowed, scores, 0.0).astype(BF16)
            out_ref[at:reach, cols] = dot(probs, head_of(v_ref, h, 0, reach), (1, 0))
            open_ref[at:reach, cols] = jnp.where(at_open, query.astype(F32), 0.0).astype(BF16)


def line_of(x):
    return jnp.sum(jnp.transpose(x), axis=0, keepdims=True)


def attend_kernel(g_hbm, local_ref, open_ref, state_ref, gain_ref, scaled_ref, sums_ref, g_ref, sems):
    def copy(i):
        rows = pl.ds(i * STEP, STEP)
        return pltpu.make_async_copy(g_hbm.at[rows], g_ref.at[rows], sems.at[i])

    for i in range(TILES):
        copy(i).start()
    states = get_state(state_ref)

    lines = [[], []]

    def put(n, i, x):
        line = line_of(x)
        lines[n] += [line[:, j * HS : (j + 1) * HS] for j in range(STEP // HS)]

    for i in range(TILES):
        at, reach = i * STEP, (i + 1) * STEP
        power = jnp.zeros((STEP, HS), F32)
        for h in range(LOCAL):
            carried = dot(head_of(open_ref, h, at, STEP), states[h], (1, 0))
            scaled = (head_of(local_ref, h, at, STEP) + carried) * gain_ref[h : h + 1, :]
            scaled_ref[at:reach, h * HS : (h + 1) * HS] = scaled
            power = power + scaled * scaled
        put(0, i, power)
    for i in range(TILES):
        copy(i).wait()
        cross = jnp.zeros((STEP, HS), F32)
        for h in range(LOCAL):
            cross = cross + head_of(scaled_ref, h, i * STEP, STEP) * head_of(g_ref, h, i * STEP, STEP).astype(F32)
        put(1, i, cross)
    total = jnp.concatenate(lines[0] + lines[1], axis=0)
    for peer in range(PEERS):
        sums_ref[peer * 2 * LINES : (peer + 1) * 2 * LINES, :] = total


def scale_and_pull(sums_ref):
    lines = 2 * LINES
    total = sums_ref[0:lines]
    for peer in range(1, PEERS):
        total = total + sums_ref[peer * lines : (peer + 1) * lines]
    width = HEADS * HS
    scale = lax.rsqrt(total[:LINES] / width + EPS)
    return scale, total[LINES:] * scale * scale * scale / width


def columns_of(lines, i):
    per = STEP // HS
    return jnp.concatenate([column_of(lines[i * per + j : i * per + j + 1]) for j in range(per)], axis=0)


def inner_kernel(scaled_ref, g_ref, open_ref, sums_ref, gain_ref, inner_ref, tail_ref):
    scale, pull = scale_and_pull(sums_ref)
    tails = [jnp.zeros((HS, HS), F32) for _ in range(LOCAL)]
    for i in range(TILES):
        at, reach = i * STEP, (i + 1) * STEP
        scales, pulls = columns_of(scale, i), columns_of(pull, i)
        for h in range(LOCAL):
            cols = slice(h * HS, (h + 1) * HS)
            grad = g_ref[at:reach, cols].astype(F32)
            inner = (gain_ref[h : h + 1, :] * (grad * scales - scaled_ref[at:reach, cols] * pulls)).astype(BF16)
            inner_ref[at:reach, cols] = inner
            tails[h] = tails[h] + dot(open_ref[at:reach, cols], inner, (0, 0))
    put_state(tail_ref, tails, CHUNK)


def attended_kernel(scaled_ref, sums_ref, out_ref):
    scale, _ = scale_and_pull(sums_ref)
    for i in range(TILES):
        at, reach = i * STEP, (i + 1) * STEP
        scales = columns_of(scale, i)
        for h in range(LOCAL):
            cols = slice(h * HS, (h + 1) * HS)
            out_ref[at:reach, cols] = (scaled_ref[at:reach, cols] * scales).astype(BF16)


def near_queries_kernel(q_ref, k_ref, v_ref, seg_ref, row_ref, inner_ref, state_ref, gq_ref, keys_ref):
    _, _, n_open, _ = marks_of(seg_ref)
    states = get_state(state_ref)
    keys_ref[...] = jnp.zeros(keys_ref.shape, F32)
    for i in range(TILES):
        at, reach = i * STEP, (i + 1) * STEP
        allowed = allowed_tile(row_ref, i)
        at_open = positions(at, STEP) < n_open
        for h in range(LOCAL):
            cols = slice(h * HS, (h + 1) * HS)
            inner = inner_ref[at:reach, cols]
            dscores = dot(inner, v_ref[:reach, cols], (1, 1))
            dprobs = jnp.where(allowed, dscores, 0.0).astype(BF16)
            grad_q = dot(dprobs, k_ref[:reach, cols], (1, 0))
            grad_q = grad_q + jnp.where(at_open, dot(inner, states[h], (1, 1)), 0.0)
            gq_ref[at:reach, cols] = grad_q.astype(BF16)
            keys_ref[:reach, cols] += dot(dprobs, q_ref[at:reach, cols], (0, 0))


def near_values_kernel(q_ref, k_ref, row_ref, inner_ref, values_ref):
    values_ref[...] = jnp.zeros(values_ref.shape, F32)
    for i in range(TILES):
        at, reach = i * STEP, (i + 1) * STEP
        allowed = allowed_tile(row_ref, i)
        for h in range(LOCAL):
            cols = slice(h * HS, (h + 1) * HS)
            scores = dot(q_ref[at:reach, cols], k_ref[:reach, cols], (1, 1))
            probs = jnp.where(allowed, scores, 0.0).astype(BF16)
            values_ref[:reach, cols] += dot(probs, inner_ref[at:reach, cols], (0, 0))


def far_kernel(
    k_hbm, v_ref, keys_ref, values_ref, back_ref, seg_ref, gk_hbm, gv_hbm, k_ref, gk_ref, gv_ref, sems
):
    def copy(n, a, b, i):
        rows = pl.ds(i * STEP, STEP)
        return pltpu.make_async_copy(a.at[rows], b.at[rows], sems.at[n, i])

    for i in range(TILES):
        copy(0, k_hbm, k_ref, i).start()
    _, _, _, start = marks_of(seg_ref)
    backs = get_state(back_ref)
    for i in range(TILES):
        at, reach = i * STEP, (i + 1) * STEP
        at_close = positions(at, STEP) >= start
        for h in range(LOCAL):
            cols = slice(h * HS, (h + 1) * HS)
            far = jnp.where(at_close, dot(v_ref[at:reach, cols], backs[h], (1, 1)), 0.0)
            gk_ref[at:reach, cols] = (keys_ref[at:reach, cols] + far).astype(BF16)
        copy(1, gk_ref, gk_hbm, i).start()
    for i in range(TILES):
        at, reach = i * STEP, (i + 1) * STEP
        at_close = positions(at, STEP) >= start
        copy(0, k_hbm, k_ref, i).wait()
        for h in range(LOCAL):
            cols = slice(h * HS, (h + 1) * HS)
            far = jnp.where(at_close, dot(k_ref[at:reach, cols], backs[h], (1, 0)), 0.0)
            gv_ref[at:reach, cols] = (values_ref[at:reach, cols] + far).astype(BF16)
        copy(2, gv_ref, gv_hbm, i).start()
    for i in range(TILES):
        copy(1, gk_ref, gk_hbm, i).wait()
        copy(2, gv_ref, gv_hbm, i).wait()


def exchange(x):
    parts = x.reshape(RING, 1, -1)
    rings = [[y * RING + z for z in range(RING)] for y in range(N_ROWS)]
    out = lax.all_to_all(parts, "ctx", 0, 0, axis_index_groups=rings, tiled=True)
    return out.reshape(x.shape)


def to_row(x, by):
    pairs = [(i, i + by * RING) for i in range(N_ROWS * RING)]
    return lax.ppermute(x, "ctx", [(a, b) for a, b in pairs if 0 <= b < N_ROWS * RING])


def over_heads(x):
    parts = x.reshape(PEERS, 1, -1)
    return lax.all_to_all(parts, "head", 0, 0, tiled=True).reshape(x.shape)


def per_device(queries, key_vectors, value_vectors, out_grad, segment_ids, head_gain):
    q, k, v, g, gain = queries, key_vectors, value_vectors, out_grad, head_gain
    seg = segment_ids.reshape(8, HS)
    row = segment_ids.reshape(1, ROWS)
    states = ((RING * CHUNK, HS), F32)
    wide, wide_half = ((ROWS, LOCAL * HS), F32), ((ROWS, LOCAL * HS), BF16)
    payload = ((RING * (CHUNK + 1), HS), F32)
    sums = ((PEERS * 2 * LINES, HS), F32)
    half_stage = pltpu.VMEM(*wide_half)
    two = [half_stage, half_stage, pltpu.SemaphoreType.DMA((2, TILES))]

    seg_stage, seg_sem = pltpu.VMEM((8, HS), jnp.int32), pltpu.SemaphoreType.DMA
    (tail,) = call(
        tail_kernel, "tail", [payload], (seg, k, v), scratch=[seg_stage, *two, seg_sem], stage=False
    )
    tails = exchange(tail)
    gains = ((LOCAL, HS), F32)
    local, q_open, gains = call(
        local_kernel, "local", [wide, wide_half, gains], (q, k, v, seg, row), (gain,), [SMEM]
    )
    carry = ((CHUNK + 8, HS), F32)
    row_end, marks = call(row_end_kernel, "row_end", [carry, ((RING, HS), F32)], near=(tails,))
    (before,) = call(before_kernel, "before", [states], near=(tails, marks, to_row(row_end, 1)))
    state_in = exchange(before)
    scaled, part = call(
        attend_kernel,
        "attend",
        [wide, sums],
        (g,),
        (local, q_open, state_in, gains),
        scratch=[half_stage, pltpu.SemaphoreType.DMA((TILES,))],
        stage=False,
    )
    total = over_heads(part)
    inner, back_tail = call(
        inner_kernel, "inner", [wide_half, states], (), (scaled, g, q_open, total, gains)
    )
    back_tails = exchange(back_tail)
    (attended,) = call(attended_kernel, "attended", [wide_half], near=(scaled, total))
    (near_v,) = call(near_values_kernel, "near_values", [wide], (q, k, row), (inner,))
    grad_q, near_k = call(
        near_queries_kernel, "near_queries", [wide_half, wide], (q, k, v, seg, row), (inner, state_in)
    )
    (row_start,) = call(row_start_kernel, "row_start", [carry], near=(back_tails, marks))
    (after,) = call(after_kernel, "after", [states], near=(back_tails, marks, to_row(row_start, -1)))
    state_grad = exchange(after)
    grad_k, grad_v = call(
        far_kernel,
        "far",
        [wide_half, wide_half],
        (k,),
        (v, near_k, near_v, state_grad, seg),
        out_far=2,
        scratch=[half_stage, half_stage, half_stage, pltpu.SemaphoreType.DMA((3, TILES))],
        stage=False,
    )
    return attended, grad_q, grad_k, grad_v


def solution(mesh):
    both = P("ctx", "head")
    return jax.shard_map(
        per_device,
        mesh=mesh,
        in_specs=(both, both, both, both, P("ctx"), P("head")),
        out_specs=(both, both, both, both),
        check_vma=False,
    )
```

```python
import jax
import jax.numpy as jnp
from jax import lax
from jax.experimental import pallas as pl
from jax.experimental.pallas import tpu as pltpu
from jax.sharding import PartitionSpec as P

HEADS = 16
HS = 128
EPS = 1e-05

ROWS = 1024
LOCAL = 2
RING = 16
N_ROWS = 4
STEP = 256
WIDE_STEP = 512
TILES = ROWS // STEP
CHUNK = LOCAL * HS // RING

PEERS = 8
LINES = ROWS // HS

VMEM = pl.BlockSpec(memory_space=pltpu.VMEM)
SMEM = pl.BlockSpec(memory_space=pltpu.SMEM)
HBM = pl.BlockSpec(memory_space=pltpu.HBM)
F32 = jnp.float32
BF16 = jnp.bfloat16


def dot(a, b, over):
    return lax.dot_general(
        a, b, (((over[0],), (over[1],)), ((), ())), preferred_element_type=F32
    )


def thirds(x):
    high = x.astype(BF16)
    rest = x - high.astype(F32)
    middle = rest.astype(BF16)
    return [high, middle, (rest - middle.astype(F32)).astype(BF16)]


def together(pairs, sems):
    copies = [pltpu.make_async_copy(a, b, sems.at[i]) for i, (a, b) in enumerate(pairs)]
    for copy in copies:
        copy.start()
    for copy in copies:
        copy.wait()


def staged(kernel, n_in, n_mid, n_out):
    def run(*refs):
        given, rest = refs[:n_in], list(refs[n_in:])
        sems = rest.pop()
        given_held, out_held = rest[n_mid + n_out :][:n_in], rest[n_mid + n_out :][n_in:]
        middle, out = rest[:n_mid], rest[n_mid : n_mid + n_out]
        together(zip(given, given_held), sems)
        kernel(*given_held, *middle, *out_held)
        together(zip(out_held, out), sems)

    return run


def call(kernel, name, outs, far=(), near=(), specs=None, out_far=0, scratch=(), stage=True):
    far = [pltpu.with_memory_space_constraint(x, pltpu.HBM) for x in far]
    if stage and (far or out_far):
        held_outs = outs[len(outs) - out_far :]
        kernel = staged(kernel, len(far), len(near) + len(outs) - out_far, out_far)
        scratch = [pltpu.VMEM(x.shape, x.dtype) for x in far]
        scratch += [pltpu.VMEM(*held) for held in held_outs]
        scratch += [pltpu.SemaphoreType.DMA((len(far) + out_far,))]
    return pl.pallas_call(
        kernel,
        name=name,
        out_shape=[jax.ShapeDtypeStruct(shape, dtype) for shape, dtype in outs],
        in_specs=[HBM] * len(far) + (specs or [VMEM] * len(near)),
        out_specs=[VMEM] * (len(outs) - out_far) + [HBM] * out_far,
        scratch_shapes=list(scratch),
        compiler_params=pltpu.CompilerParams(vmem_limit_bytes=16 << 20),
    )(*far, *near)


def marks_of(seg_ref):
    seg = seg_ref[...].astype(F32)
    opening, closing = jnp.min(seg), jnp.max(seg)
    n_open = jnp.sum(jnp.where(seg == opening, 1.0, 0.0)).astype(jnp.int32)
    n_close = jnp.sum(jnp.where(seg == closing, 1.0, 0.0)).astype(jnp.int32)
    return opening, closing, n_open, ROWS - n_close


def head_of(ref, h, start=0, size=ROWS):
    return ref[start : start + size, h * HS : (h + 1) * HS]


def positions(start, size):
    return start + lax.broadcasted_iota(jnp.int32, (size, HS), 0)


def put_state(out_ref, states, stride):
    flat = jnp.concatenate(states, axis=0)
    for r in range(CHUNK):
        out_ref[pl.ds(r, RING, stride=stride), :] = flat[r * RING : (r + 1) * RING]


def get_state(ref):
    flat = jnp.concatenate([ref[pl.ds(r, RING, stride=CHUNK), :] for r in range(CHUNK)], axis=0)
    return [flat[h * HS : (h + 1) * HS].astype(BF16) for h in range(LOCAL)]


TAIL_TILES = 2
TAIL_STEP = ROWS // TAIL_TILES


def tail_kernel(seg_hbm, k_hbm, v_hbm, out_ref, seg_ref, k_ref, v_ref, sems, seg_sem):
    def copies(i):
        rows = pl.ds(i * TAIL_STEP, TAIL_STEP)
        return [
            pltpu.make_async_copy(k_hbm.at[rows], k_ref.at[rows], sems.at[0, i]),
            pltpu.make_async_copy(v_hbm.at[rows], v_ref.at[rows], sems.at[1, i]),
        ]

    seg_copy = pltpu.make_async_copy(seg_hbm, seg_ref, seg_sem)
    seg_copy.start()
    for i in range(TAIL_TILES):
        for copy in copies(i):
            copy.start()
    seg_copy.wait()
    opening, closing, _, start = marks_of(seg_ref)
    lane = lax.broadcasted_iota(jnp.int32, (RING, HS), 1)
    out_ref[pl.ds(CHUNK, RING, stride=CHUNK + 1), :] = jnp.where(lane == 0, opening, closing) + 1.0
    tails = [jnp.zeros((HS, HS), F32) for _ in range(LOCAL)]
    for i in range(TAIL_TILES):
        for copy in copies(i):
            copy.wait()
        at_close = positions(i * TAIL_STEP, TAIL_STEP) >= start
        for h in range(LOCAL):
            keys = head_of(k_ref, h, i * TAIL_STEP, TAIL_STEP).astype(F32)
            keys = jnp.where(at_close, keys, 0.0).astype(BF16)
            tails[h] = tails[h] + dot(keys, head_of(v_ref, h, i * TAIL_STEP, TAIL_STEP), (0, 0))
    put_state(out_ref, tails, CHUNK + 1)


def chunks_of(x_ref, stride):
    return jnp.concatenate([x_ref[pl.ds(r, RING, stride=stride), :] for r in range(CHUNK)], axis=1)


def summed(chosen, x, out_ref, stride):
    chosen = jnp.where(chosen, 1.0, 0.0).astype(BF16)
    y = dot(jnp.concatenate([chosen] * 3, axis=1), jnp.concatenate(thirds(x), axis=0), (1, 0))
    for r in range(CHUNK):
        own = y[:, r * HS : (r + 1) * HS]
        if stride:
            out_ref[pl.ds(r, RING, stride=stride), :] = own
        else:
            out_ref[r : r + 1, :] = own[0:1]


def iotas(down, along):
    return [lax.broadcasted_iota(jnp.int32, (down, along), d) for d in range(2)]


def as_row(column):
    n = column.shape[0]
    down, along = iotas(n, n)
    return jnp.sum(jnp.where(down == along, column, 0.0), axis=0, keepdims=True)


def row_end_kernel(x_ref, out_ref, marks_ref):
    marks = x_ref[pl.ds(CHUNK, RING, stride=CHUNK + 1), :]
    marks_ref[...] = marks
    closing = marks[RING - 1 : RING, 1:2]
    chosen = jnp.broadcast_to(as_row(marks[:, 1:2]) == closing, (8, RING))
    summed(chosen, chunks_of(x_ref, CHUNK + 1), out_ref, 0)
    out_ref[CHUNK:, :] = jnp.broadcast_to(closing, (8, HS))


def row_start_kernel(x_ref, marks_ref, out_ref):
    opening = marks_ref[0:1, 0:1]
    chosen = jnp.broadcast_to(as_row(marks_ref[:, 0:1]) == opening, (8, RING))
    summed(chosen, chunks_of(x_ref, CHUNK), out_ref, 0)
    out_ref[CHUNK:, :] = jnp.broadcast_to(opening, (8, HS))


def before_kernel(x_ref, marks_ref, out_ref):
    down, along = iotas(RING, RING)
    chosen = (as_row(marks_ref[:, 1:2]) == marks_ref[:, 0:1]) & (along < down)
    summed(chosen, chunks_of(x_ref, CHUNK + 1), out_ref, CHUNK)


def after_kernel(x_ref, marks_ref, out_ref):
    down, along = iotas(RING, RING)
    chosen = (as_row(marks_ref[:, 0:1]) == marks_ref[:, 1:2]) & (along > down)
    summed(chosen, chunks_of(x_ref, CHUNK), out_ref, CHUNK)


def carried_over(side):
    def kernel(x_ref, marks_ref, more_ref, out_ref):
        more = more_ref[:CHUNK, :]
        mark = more_ref[CHUNK : CHUNK + 1, 0:1]
        for block in range(RING):
            joined = marks_ref[block : block + 1, side : side + 1] == mark
            rows = slice(block * CHUNK, (block + 1) * CHUNK)
            out_ref[rows, :] = x_ref[rows, :] + jnp.where(joined, more, 0.0)

    return kernel


def column_of(row):
    return jnp.transpose(jnp.broadcast_to(row, (HS, row.shape[1])))


def allowed_tile(seg_ref, i):
    reach = (i + 1) * STEP
    own = column_of(seg_ref[:, i * STEP : reach].astype(F32))
    same = jnp.concatenate([own] * (reach // HS), axis=1) == seg_ref[:, :reach].astype(F32)
    at = i * STEP + lax.broadcasted_iota(jnp.int32, (STEP, reach), 0)
    return same & (lax.broadcasted_iota(jnp.int32, (STEP, reach), 1) <= at)


def local_kernel(q_ref, k_ref, v_ref, seg_ref, row_ref, gain_ref, out_ref, open_ref, gains_ref):
    _, _, n_open, _ = marks_of(seg_ref)
    for h in range(LOCAL):
        gains_ref[h : h + 1, :] = jnp.full((1, HS), gain_ref[h], F32)
    for i in range(TILES):
        at, reach = i * STEP, (i + 1) * STEP
        allowed = allowed_tile(row_ref, i)
        at_open = positions(at, STEP) < n_open
        for h in range(LOCAL):
            cols = slice(h * HS, (h + 1) * HS)
            query = q_ref[at:reach, cols]
            scores = dot(query, head_of(k_ref, h, 0, reach), (1, 1))
            probs = jnp.where(allowed, scores, 0.0).astype(BF16)
            out_ref[at:reach, cols] = dot(probs, head_of(v_ref, h, 0, reach), (1, 0))
            open_ref[at:reach, cols] = jnp.where(at_open, query.astype(F32), 0.0).astype(BF16)


def line_of(x):
    return jnp.sum(jnp.transpose(x), axis=0, keepdims=True)


def attend_kernel(g_hbm, local_ref, open_ref, state_ref, gain_ref, scaled_ref, sums_ref, g_ref, sems):
    def copy(i):
        rows = pl.ds(i * WIDE_STEP, WIDE_STEP)
        return pltpu.make_async_copy(g_hbm.at[rows], g_ref.at[rows], sems.at[i])

    for i in range((ROWS // WIDE_STEP)):
        copy(i).start()
    states = get_state(state_ref)

    lines = [[], []]

    def put(n, i, x):
        line = line_of(x)
        lines[n] += [line[:, j * HS : (j + 1) * HS] for j in range(WIDE_STEP // HS)]

    for i in range((ROWS // WIDE_STEP)):
        at, reach = i * WIDE_STEP, (i + 1) * WIDE_STEP
        power = jnp.zeros((WIDE_STEP, HS), F32)
        for h in range(LOCAL):
            carried = dot(head_of(open_ref, h, at, WIDE_STEP), states[h], (1, 0))
            scaled = (head_of(local_ref, h, at, WIDE_STEP) + carried) * gain_ref[h : h + 1, :]
            scaled_ref[at:reach, h * HS : (h + 1) * HS] = scaled
            power = power + scaled * scaled
        put(0, i, power)
    for i in range((ROWS // WIDE_STEP)):
        copy(i).wait()
        cross = jnp.zeros((WIDE_STEP, HS), F32)
        for h in range(LOCAL):
            cross = cross + head_of(scaled_ref, h, i * WIDE_STEP, WIDE_STEP) * head_of(g_ref, h, i * WIDE_STEP, WIDE_STEP).astype(F32)
        put(1, i, cross)
    total = jnp.concatenate(lines[0] + lines[1], axis=0)
    for peer in range(PEERS):
        sums_ref[peer * 2 * LINES : (peer + 1) * 2 * LINES, :] = total


def scale_and_pull(sums_ref):
    lines = 2 * LINES
    total = sums_ref[0:lines]
    for peer in range(1, PEERS):
        total = total + sums_ref[peer * lines : (peer + 1) * lines]
    width = HEADS * HS
    scale = lax.rsqrt(total[:LINES] / width + EPS)
    return scale, total[LINES:] * scale * scale * scale / width


def columns_of(lines, i):
    per = STEP // HS
    return jnp.concatenate([column_of(lines[i * per + j : i * per + j + 1]) for j in range(per)], axis=0)


def inner_kernel(scaled_ref, g_ref, open_ref, sums_ref, gain_ref, inner_ref, tail_ref):
    scale, pull = scale_and_pull(sums_ref)
    tails = [jnp.zeros((HS, HS), F32) for _ in range(LOCAL)]
    for i in range(TILES):
        at, reach = i * STEP, (i + 1) * STEP
        scales, pulls = columns_of(scale, i), columns_of(pull, i)
        for h in range(LOCAL):
            cols = slice(h * HS, (h + 1) * HS)
            grad = g_ref[at:reach, cols].astype(F32)
            inner = (gain_ref[h : h + 1, :] * (grad * scales - scaled_ref[at:reach, cols] * pulls)).astype(BF16)
            inner_ref[at:reach, cols] = inner
            tails[h] = tails[h] + dot(open_ref[at:reach, cols], inner, (0, 0))
    put_state(tail_ref, tails, CHUNK)


def attended_kernel(scaled_ref, sums_ref, out_ref):
    scale, _ = scale_and_pull(sums_ref)
    for i in range(TILES):
        at, reach = i * STEP, (i + 1) * STEP
        scales = columns_of(scale, i)
        for h in range(LOCAL):
            cols = slice(h * HS, (h + 1) * HS)
            out_ref[at:reach, cols] = (scaled_ref[at:reach, cols] * scales).astype(BF16)


def at_close_only(ref, start, out_ref):
    for h in range(LOCAL):
        x = jnp.where(positions(0, ROWS) >= start, head_of(ref, h).astype(F32), 0.0)
        out_ref[:, h * HS : (h + 1) * HS] = x.astype(BF16)


def near_queries_kernel(
    q_ref, k_ref, v_ref, seg_ref, row_ref, inner_ref, state_ref, gq_ref, keys_ref, closing_ref
):
    _, _, n_open, start = marks_of(seg_ref)
    at_close_only(v_ref, start, closing_ref)
    states = get_state(state_ref)
    keys_ref[...] = jnp.zeros(keys_ref.shape, F32)
    for i in range(TILES):
        at, reach = i * STEP, (i + 1) * STEP
        allowed = allowed_tile(row_ref, i)
        at_open = positions(at, STEP) < n_open
        for h in range(LOCAL):
            cols = slice(h * HS, (h + 1) * HS)
            inner = inner_ref[at:reach, cols]
            dscores = dot(inner, v_ref[:reach, cols], (1, 1))
            dprobs = jnp.where(allowed, dscores, 0.0).astype(BF16)
            grad_q = dot(dprobs, k_ref[:reach, cols], (1, 0))
            grad_q = grad_q + jnp.where(at_open, dot(inner, states[h], (1, 1)), 0.0)
            gq_ref[at:reach, cols] = grad_q.astype(BF16)
            keys_ref[:reach, cols] += dot(dprobs, q_ref[at:reach, cols], (0, 0))


def near_values_kernel(q_ref, k_ref, seg_ref, row_ref, inner_ref, values_ref, closing_ref):
    _, _, _, start = marks_of(seg_ref)
    at_close_only(k_ref, start, closing_ref)
    values_ref[...] = jnp.zeros(values_ref.shape, F32)
    for i in range(TILES):
        at, reach = i * STEP, (i + 1) * STEP
        allowed = allowed_tile(row_ref, i)
        for h in range(LOCAL):
            cols = slice(h * HS, (h + 1) * HS)
            scores = dot(q_ref[at:reach, cols], k_ref[:reach, cols], (1, 1))
            probs = jnp.where(allowed, scores, 0.0).astype(BF16)
            values_ref[:reach, cols] += dot(probs, inner_ref[at:reach, cols], (0, 0))


def far_kernel(
    k_hbm, v_ref, keys_ref, values_ref, back_ref, gk_hbm, gv_hbm, k_ref, gk_ref, gv_ref, sems, k_sem
):
    fetch = pltpu.make_async_copy(k_hbm, k_ref, k_sem)
    fetch.start()
    backs = get_state(back_ref)
    copies = []
    for i in range(ROWS // WIDE_STEP):
        at, reach = i * WIDE_STEP, (i + 1) * WIDE_STEP
        rows = pl.ds(at, WIDE_STEP)
        for h in range(LOCAL):
            cols = slice(h * HS, (h + 1) * HS)
            far = dot(v_ref[at:reach, cols], backs[h], (1, 1))
            gk_ref[at:reach, cols] = (keys_ref[at:reach, cols] + far).astype(BF16)
        copies.append(pltpu.make_async_copy(gk_ref.at[rows], gk_hbm.at[rows], sems.at[0, i]))
        copies[-1].start()
    fetch.wait()
    for i in range(ROWS // WIDE_STEP):
        at, reach = i * WIDE_STEP, (i + 1) * WIDE_STEP
        rows = pl.ds(at, WIDE_STEP)
        for h in range(LOCAL):
            cols = slice(h * HS, (h + 1) * HS)
            far = dot(k_ref[at:reach, cols], backs[h], (1, 0))
            gv_ref[at:reach, cols] = (values_ref[at:reach, cols] + far).astype(BF16)
        copies.append(pltpu.make_async_copy(gv_ref.at[rows], gv_hbm.at[rows], sems.at[1, i]))
        copies[-1].start()
    for copy in copies:
        copy.wait()


def exchange(x):
    parts = x.reshape(RING, 1, -1)
    rings = [[y * RING + z for z in range(RING)] for y in range(N_ROWS)]
    out = lax.all_to_all(parts, "ctx", 0, 0, axis_index_groups=rings, tiled=True)
    return out.reshape(x.shape)


def to_row(x, by):
    pairs = [(i, i + by * RING) for i in range(N_ROWS * RING)]
    return lax.ppermute(x, "ctx", [(a, b) for a, b in pairs if 0 <= b < N_ROWS * RING])


def over_heads(x):
    parts = x.reshape(PEERS, 1, -1)
    return lax.all_to_all(parts, "head", 0, 0, tiled=True).reshape(x.shape)


def per_device(queries, key_vectors, value_vectors, out_grad, segment_ids, head_gain):
    q, k, v, g, gain = queries, key_vectors, value_vectors, out_grad, head_gain
    seg = segment_ids.reshape(8, HS)
    row = segment_ids.reshape(1, ROWS)
    states = ((RING * CHUNK, HS), F32)
    wide, wide_half = ((ROWS, LOCAL * HS), F32), ((ROWS, LOCAL * HS), BF16)
    payload = ((RING * (CHUNK + 1), HS), F32)
    sums = ((PEERS * 2 * LINES, HS), F32)
    half_stage = pltpu.VMEM(*wide_half)
    two = [half_stage, half_stage, pltpu.SemaphoreType.DMA((2, TILES))]

    seg_stage, seg_sem = pltpu.VMEM((8, HS), jnp.int32), pltpu.SemaphoreType.DMA
    (tail,) = call(
        tail_kernel, "tail", [payload], (seg, k, v), scratch=[seg_stage, *two, seg_sem], stage=False
    )
    tails = exchange(tail)
    gains = ((LOCAL, HS), F32)
    local, q_open, gains = call(
        local_kernel, "local", [wide, wide_half, gains], (q, k, v, seg, row), (gain,), [SMEM]
    )
    carry = ((CHUNK + 8, HS), F32)
    row_end, marks = call(row_end_kernel, "row_end", [carry, ((RING, HS), F32)], near=(tails,))
    (before,) = call(before_kernel, "before", [states], near=(tails, marks))
    (before,) = call(carried_over(0), "carry_on", [states], near=(before, marks, to_row(row_end, 1)))
    state_in = exchange(before)
    scaled, part = call(
        attend_kernel,
        "attend",
        [wide, sums],
        (g,),
        (local, q_open, state_in, gains),
        scratch=[half_stage, pltpu.SemaphoreType.DMA((TILES,))],
        stage=False,
    )
    total = over_heads(part)
    inner, back_tail = call(
        inner_kernel, "inner", [wide_half, states], (), (scaled, g, q_open, total, gains)
    )
    back_tails = exchange(back_tail)
    (attended,) = call(attended_kernel, "attended", [wide_half], near=(scaled, total))
    near_v, k_close = call(near_values_kernel, "near_values", [wide, wide_half], (q, k, seg, row), (inner,), out_far=1)
    grad_q, near_k, v_close = call(
        near_queries_kernel, "near_queries", [wide_half, wide, wide_half], (q, k, v, seg, row), (inner, state_in)
    )
    (row_start,) = call(row_start_kernel, "row_start", [carry], near=(back_tails, marks))
    (after,) = call(after_kernel, "after", [states], near=(back_tails, marks))
    (after,) = call(carried_over(1), "carry_back", [states], near=(after, marks, to_row(row_start, -1)))
    state_grad = exchange(after)
    grad_k, grad_v = call(
        far_kernel,
        "far",
        [wide_half, wide_half],
        (k_close,),
        (v_close, near_k, near_v, state_grad),
        out_far=2,
        scratch=[half_stage, *two, pltpu.SemaphoreType.DMA],
        stage=False,
    )
    return attended, grad_q, grad_k, grad_v


def solution(mesh):
    both = P("ctx", "head")
    return jax.shard_map(
        per_device,
        mesh=mesh,
        in_specs=(both, both, both, both, P("ctx"), P("head")),
        out_specs=(both, both, both, both),
        check_vma=False,
    )
```

```python
import jax
import jax.numpy as jnp
from jax import lax
from jax.experimental import pallas as pl
from jax.experimental.pallas import tpu as pltpu
from jax.sharding import PartitionSpec as P

HEADS = 16
HS = 128
EPS = 1e-05

ROWS = 1024
LOCAL = 2
RING = 16
N_ROWS = 4
STEP = 256
WIDE_STEP = 512
TILES = ROWS // STEP
CHUNK = LOCAL * HS // RING

PEERS = 8
LINES = ROWS // HS

VMEM = pl.BlockSpec(memory_space=pltpu.VMEM)
SMEM = pl.BlockSpec(memory_space=pltpu.SMEM)
HBM = pl.BlockSpec(memory_space=pltpu.HBM)
F32 = jnp.float32
BF16 = jnp.bfloat16


def dot(a, b, over):
    return lax.dot_general(
        a, b, (((over[0],), (over[1],)), ((), ())), preferred_element_type=F32
    )


def thirds(x):
    high = x.astype(BF16)
    rest = x - high.astype(F32)
    middle = rest.astype(BF16)
    return [high, middle, (rest - middle.astype(F32)).astype(BF16)]


def together(pairs, sems):
    copies = [pltpu.make_async_copy(a, b, sems.at[i]) for i, (a, b) in enumerate(pairs)]
    for copy in copies:
        copy.start()
    for copy in copies:
        copy.wait()


def staged(kernel, n_in, n_mid, n_out):
    def run(*refs):
        given, rest = refs[:n_in], list(refs[n_in:])
        sems = rest.pop()
        given_held, out_held = rest[n_mid + n_out :][:n_in], rest[n_mid + n_out :][n_in:]
        middle, out = rest[:n_mid], rest[n_mid : n_mid + n_out]
        together(zip(given, given_held), sems)
        kernel(*given_held, *middle, *out_held)
        together(zip(out_held, out), sems)

    return run


def call(kernel, name, outs, far=(), near=(), specs=None, out_far=0, scratch=(), stage=True):
    far = [pltpu.with_memory_space_constraint(x, pltpu.HBM) for x in far]
    if stage and (far or out_far):
        held_outs = outs[len(outs) - out_far :]
        kernel = staged(kernel, len(far), len(near) + len(outs) - out_far, out_far)
        scratch = [pltpu.VMEM(x.shape, x.dtype) for x in far]
        scratch += [pltpu.VMEM(*held) for held in held_outs]
        scratch += [pltpu.SemaphoreType.DMA((len(far) + out_far,))]
    return pl.pallas_call(
        kernel,
        name=name,
        out_shape=[jax.ShapeDtypeStruct(shape, dtype) for shape, dtype in outs],
        in_specs=[HBM] * len(far) + (specs or [VMEM] * len(near)),
        out_specs=[VMEM] * (len(outs) - out_far) + [HBM] * out_far,
        scratch_shapes=list(scratch),
        compiler_params=pltpu.CompilerParams(vmem_limit_bytes=16 << 20),
    )(*far, *near)


def marks_of(seg_ref):
    seg = seg_ref[...].astype(F32)
    opening, closing = jnp.min(seg), jnp.max(seg)
    n_open = jnp.sum(jnp.where(seg == opening, 1.0, 0.0)).astype(jnp.int32)
    n_close = jnp.sum(jnp.where(seg == closing, 1.0, 0.0)).astype(jnp.int32)
    return opening, closing, n_open, ROWS - n_close


def head_of(ref, h, start=0, size=ROWS):
    return ref[start : start + size, h * HS : (h + 1) * HS]


def positions(start, size):
    return start + lax.broadcasted_iota(jnp.int32, (size, HS), 0)


def put_state(out_ref, states, stride):
    flat = jnp.concatenate(states, axis=0)
    for r in range(CHUNK):
        out_ref[pl.ds(r, RING, stride=stride), :] = flat[r * RING : (r + 1) * RING]


def get_state(ref):
    flat = jnp.concatenate([ref[pl.ds(r, RING, stride=CHUNK), :] for r in range(CHUNK)], axis=0)
    return [flat[h * HS : (h + 1) * HS].astype(BF16) for h in range(LOCAL)]


TAIL_TILES = 2
TAIL_STEP = ROWS // TAIL_TILES


def tail_kernel(seg_hbm, k_hbm, v_hbm, out_ref, seg_ref, k_ref, v_ref, sems, seg_sem):
    def copies(i):
        rows = pl.ds(i * TAIL_STEP, TAIL_STEP)
        return [
            pltpu.make_async_copy(k_hbm.at[rows], k_ref.at[rows], sems.at[0, i]),
            pltpu.make_async_copy(v_hbm.at[rows], v_ref.at[rows], sems.at[1, i]),
        ]

    seg_copy = pltpu.make_async_copy(seg_hbm, seg_ref, seg_sem)
    seg_copy.start()
    for i in range(TAIL_TILES):
        for copy in copies(i):
            copy.start()
    seg_copy.wait()
    opening, closing, _, start = marks_of(seg_ref)
    lane = lax.broadcasted_iota(jnp.int32, (RING, HS), 1)
    out_ref[pl.ds(CHUNK, RING, stride=CHUNK + 1), :] = jnp.where(lane == 0, opening, closing) + 1.0
    tails = [jnp.zeros((HS, HS), F32) for _ in range(LOCAL)]
    for i in range(TAIL_TILES):
        for copy in copies(i):
            copy.wait()
        at_close = positions(i * TAIL_STEP, TAIL_STEP) >= start
        for h in range(LOCAL):
            keys = head_of(k_ref, h, i * TAIL_STEP, TAIL_STEP).astype(F32)
            keys = jnp.where(at_close, keys, 0.0).astype(BF16)
            tails[h] = tails[h] + dot(keys, head_of(v_ref, h, i * TAIL_STEP, TAIL_STEP), (0, 0))
    put_state(out_ref, tails, CHUNK + 1)


def chunks_of(x_ref, stride):
    return jnp.concatenate([x_ref[pl.ds(r, RING, stride=stride), :] for r in range(CHUNK)], axis=1)


def summed(chosen, x, out_ref, stride):
    chosen = jnp.where(chosen, 1.0, 0.0).astype(BF16)
    y = dot(jnp.concatenate([chosen] * 3, axis=1), jnp.concatenate(thirds(x), axis=0), (1, 0))
    for r in range(CHUNK):
        own = y[:, r * HS : (r + 1) * HS]
        if stride:
            out_ref[pl.ds(r, RING, stride=stride), :] = own
        else:
            out_ref[r : r + 1, :] = own[0:1]


def iotas(down, along):
    return [lax.broadcasted_iota(jnp.int32, (down, along), d) for d in range(2)]


def as_row(column):
    n = column.shape[0]
    down, along = iotas(n, n)
    return jnp.sum(jnp.where(down == along, column, 0.0), axis=0, keepdims=True)


def row_end_kernel(x_ref, out_ref, marks_ref):
    marks = x_ref[pl.ds(CHUNK, RING, stride=CHUNK + 1), :]
    marks_ref[...] = marks
    closing = marks[RING - 1 : RING, 1:2]
    chosen = jnp.broadcast_to(as_row(marks[:, 1:2]) == closing, (8, RING))
    summed(chosen, chunks_of(x_ref, CHUNK + 1), out_ref, 0)
    out_ref[CHUNK:, :] = jnp.broadcast_to(closing, (8, HS))


def row_start_kernel(x_ref, marks_ref, out_ref):
    opening = marks_ref[0:1, 0:1]
    chosen = jnp.broadcast_to(as_row(marks_ref[:, 0:1]) == opening, (8, RING))
    summed(chosen, chunks_of(x_ref, CHUNK), out_ref, 0)
    out_ref[CHUNK:, :] = jnp.broadcast_to(opening, (8, HS))


def before_kernel(x_ref, marks_ref, out_ref):
    down, along = iotas(RING, RING)
    chosen = (as_row(marks_ref[:, 1:2]) == marks_ref[:, 0:1]) & (along < down)
    summed(chosen, chunks_of(x_ref, CHUNK + 1), out_ref, CHUNK)


def after_kernel(x_ref, marks_ref, out_ref):
    down, along = iotas(RING, RING)
    chosen = (as_row(marks_ref[:, 0:1]) == marks_ref[:, 1:2]) & (along > down)
    summed(chosen, chunks_of(x_ref, CHUNK), out_ref, CHUNK)


def carried_over(side):
    def kernel(x_ref, marks_ref, more_ref, out_ref):
        more = more_ref[:CHUNK, :]
        mark = more_ref[CHUNK : CHUNK + 1, 0:1]
        for block in range(RING):
            joined = marks_ref[block : block + 1, side : side + 1] == mark
            rows = slice(block * CHUNK, (block + 1) * CHUNK)
            out_ref[rows, :] = x_ref[rows, :] + jnp.where(joined, more, 0.0)

    return kernel


def column_of(row):
    return jnp.transpose(jnp.broadcast_to(row, (HS, row.shape[1])))


def allowed_tile(seg_ref, i):
    reach = (i + 1) * STEP
    own = column_of(seg_ref[:, i * STEP : reach].astype(F32))
    same = jnp.concatenate([own] * (reach // HS), axis=1) == seg_ref[:, :reach].astype(F32)
    at = i * STEP + lax.broadcasted_iota(jnp.int32, (STEP, reach), 0)
    return same & (lax.broadcasted_iota(jnp.int32, (STEP, reach), 1) <= at)


def local_kernel(q_ref, k_ref, v_ref, seg_ref, row_ref, gain_ref, out_ref, open_ref, gains_ref):
    _, _, n_open, _ = marks_of(seg_ref)
    for h in range(LOCAL):
        gains_ref[h : h + 1, :] = jnp.full((1, HS), gain_ref[h], F32)
    for i in range(TILES):
        at, reach = i * STEP, (i + 1) * STEP
        allowed = allowed_tile(row_ref, i)
        at_open = positions(at, STEP) < n_open
        for h in range(LOCAL):
            cols = slice(h * HS, (h + 1) * HS)
            query = q_ref[at:reach, cols]
            scores = dot(query, head_of(k_ref, h, 0, reach), (1, 1))
            probs = jnp.where(allowed, scores, 0.0).astype(BF16)
            out_ref[at:reach, cols] = dot(probs, head_of(v_ref, h, 0, reach), (1, 0))
            open_ref[at:reach, cols] = jnp.where(at_open, query.astype(F32), 0.0).astype(BF16)


def line_of(x):
    return jnp.sum(jnp.transpose(x), axis=0, keepdims=True)


def attend_kernel(g_hbm, local_ref, open_ref, state_ref, gain_ref, scaled_ref, sums_ref, g_ref, sems):
    def copy(i):
        rows = pl.ds(i * WIDE_STEP, WIDE_STEP)
        return pltpu.make_async_copy(g_hbm.at[rows], g_ref.at[rows], sems.at[i])

    for i in range((ROWS // WIDE_STEP)):
        copy(i).start()
    states = get_state(state_ref)

    lines = [[], []]

    def put(n, i, x):
        line = line_of(x)
        lines[n] += [line[:, j * HS : (j + 1) * HS] for j in range(WIDE_STEP // HS)]

    for i in range((ROWS // WIDE_STEP)):
        at, reach = i * WIDE_STEP, (i + 1) * WIDE_STEP
        power = jnp.zeros((WIDE_STEP, HS), F32)
        for h in range(LOCAL):
            carried = dot(head_of(open_ref, h, at, WIDE_STEP), states[h], (1, 0))
            scaled = (head_of(local_ref, h, at, WIDE_STEP) + carried) * gain_ref[h : h + 1, :]
            scaled_ref[at:reach, h * HS : (h + 1) * HS] = scaled
            power = power + scaled * scaled
        put(0, i, power)
    for i in range((ROWS // WIDE_STEP)):
        copy(i).wait()
        cross = jnp.zeros((WIDE_STEP, HS), F32)
        for h in range(LOCAL):
            cross = cross + head_of(scaled_ref, h, i * WIDE_STEP, WIDE_STEP) * head_of(g_ref, h, i * WIDE_STEP, WIDE_STEP).astype(F32)
        put(1, i, cross)
    total = jnp.concatenate(lines[0] + lines[1], axis=0)
    for peer in range(PEERS):
        sums_ref[peer * 2 * LINES : (peer + 1) * 2 * LINES, :] = total


def scale_and_pull(sums_ref):
    lines = 2 * LINES
    total = sums_ref[0:lines]
    for peer in range(1, PEERS):
        total = total + sums_ref[peer * lines : (peer + 1) * lines]
    width = HEADS * HS
    scale = lax.rsqrt(total[:LINES] / width + EPS)
    return scale, total[LINES:] * scale * scale * scale / width


def columns_of(lines, i):
    per = STEP // HS
    return jnp.concatenate([column_of(lines[i * per + j : i * per + j + 1]) for j in range(per)], axis=0)


def inner_kernel(scaled_ref, g_ref, open_ref, sums_ref, gain_ref, inner_ref, tail_ref):
    scale, pull = scale_and_pull(sums_ref)
    tails = [jnp.zeros((HS, HS), F32) for _ in range(LOCAL)]
    for i in range(TILES):
        at, reach = i * STEP, (i + 1) * STEP
        scales, pulls = columns_of(scale, i), columns_of(pull, i)
        for h in range(LOCAL):
            cols = slice(h * HS, (h + 1) * HS)
            grad = g_ref[at:reach, cols].astype(F32)
            inner = (gain_ref[h : h + 1, :] * (grad * scales - scaled_ref[at:reach, cols] * pulls)).astype(BF16)
            inner_ref[at:reach, cols] = inner
            tails[h] = tails[h] + dot(open_ref[at:reach, cols], inner, (0, 0))
    put_state(tail_ref, tails, CHUNK)


def attended_kernel(scaled_ref, sums_ref, out_ref):
    scale, _ = scale_and_pull(sums_ref)
    for i in range(TILES):
        at, reach = i * STEP, (i + 1) * STEP
        scales = columns_of(scale, i)
        for h in range(LOCAL):
            cols = slice(h * HS, (h + 1) * HS)
            out_ref[at:reach, cols] = (scaled_ref[at:reach, cols] * scales).astype(BF16)


def at_close_only(ref, start, out_ref):
    for h in range(LOCAL):
        x = jnp.where(positions(0, ROWS) >= start, head_of(ref, h).astype(F32), 0.0)
        out_ref[:, h * HS : (h + 1) * HS] = x.astype(BF16)


def near_queries_kernel(
    q_ref, k_ref, v_ref, seg_ref, row_ref, inner_ref, state_ref, gq_ref, keys_ref, closing_ref
):
    _, _, n_open, start = marks_of(seg_ref)
    at_close_only(v_ref, start, closing_ref)
    states = get_state(state_ref)
    keys_ref[...] = jnp.zeros(keys_ref.shape, F32)
    for i in range(TILES):
        at, reach = i * STEP, (i + 1) * STEP
        allowed = allowed_tile(row_ref, i)
        at_open = positions(at, STEP) < n_open
        for h in range(LOCAL):
            cols = slice(h * HS, (h + 1) * HS)
            inner = inner_ref[at:reach, cols]
            dscores = dot(inner, v_ref[:reach, cols], (1, 1))
            dprobs = jnp.where(allowed, dscores, 0.0).astype(BF16)
            grad_q = dot(dprobs, k_ref[:reach, cols], (1, 0))
            grad_q = grad_q + jnp.where(at_open, dot(inner, states[h], (1, 1)), 0.0)
            gq_ref[at:reach, cols] = grad_q.astype(BF16)
            keys_ref[:reach, cols] += dot(dprobs, q_ref[at:reach, cols], (0, 0))


def near_values_kernel(q_ref, k_ref, seg_ref, row_ref, inner_ref, values_ref, closing_ref):
    _, _, _, start = marks_of(seg_ref)
    at_close_only(k_ref, start, closing_ref)
    values_ref[...] = jnp.zeros(values_ref.shape, F32)
    for i in range(TILES):
        at, reach = i * STEP, (i + 1) * STEP
        allowed = allowed_tile(row_ref, i)
        for h in range(LOCAL):
            cols = slice(h * HS, (h + 1) * HS)
            scores = dot(q_ref[at:reach, cols], k_ref[:reach, cols], (1, 1))
            probs = jnp.where(allowed, scores, 0.0).astype(BF16)
            values_ref[:reach, cols] += dot(probs, inner_ref[at:reach, cols], (0, 0))


def far_kernel(
    k_hbm, v_ref, keys_ref, values_ref, back_ref, gk_hbm, gv_hbm, k_ref, gk_ref, gv_ref, sems, k_sem
):
    fetch = pltpu.make_async_copy(k_hbm, k_ref, k_sem)
    fetch.start()
    backs = get_state(back_ref)
    copies = []
    for i in range(ROWS // WIDE_STEP):
        at, reach = i * WIDE_STEP, (i + 1) * WIDE_STEP
        rows = pl.ds(at, WIDE_STEP)
        for h in range(LOCAL):
            cols = slice(h * HS, (h + 1) * HS)
            far = dot(v_ref[at:reach, cols], backs[h], (1, 1))
            gk_ref[at:reach, cols] = (keys_ref[at:reach, cols] + far).astype(BF16)
        copies.append(pltpu.make_async_copy(gk_ref.at[rows], gk_hbm.at[rows], sems.at[0, i]))
        copies[-1].start()
    fetch.wait()
    for i in range(ROWS // WIDE_STEP):
        at, reach = i * WIDE_STEP, (i + 1) * WIDE_STEP
        rows = pl.ds(at, WIDE_STEP)
        for h in range(LOCAL):
            cols = slice(h * HS, (h + 1) * HS)
            far = dot(k_ref[at:reach, cols], backs[h], (1, 0))
            gv_ref[at:reach, cols] = (values_ref[at:reach, cols] + far).astype(BF16)
        copies.append(pltpu.make_async_copy(gv_ref.at[rows], gv_hbm.at[rows], sems.at[1, i]))
        copies[-1].start()
    for copy in copies:
        copy.wait()


def exchange(x):
    parts = x.reshape(RING, 1, -1)
    rings = [[y * RING + z for z in range(RING)] for y in range(N_ROWS)]
    out = lax.all_to_all(parts, "ctx", 0, 0, axis_index_groups=rings, tiled=True)
    return out.reshape(x.shape)


def to_row(x, by):
    pairs = [(i, i + by * RING) for i in range(N_ROWS * RING)]
    return lax.ppermute(x, "ctx", [(a, b) for a, b in pairs if 0 <= b < N_ROWS * RING])


def over_heads(x):
    parts = x.reshape(PEERS, 1, -1)
    return lax.all_to_all(parts, "head", 0, 0, tiled=True).reshape(x.shape)


def per_device(queries, key_vectors, value_vectors, out_grad, segment_ids, head_gain):
    q, k, v, g, gain = queries, key_vectors, value_vectors, out_grad, head_gain
    seg = segment_ids.reshape(8, HS)
    row = segment_ids.reshape(1, ROWS)
    states = ((RING * CHUNK, HS), F32)
    wide, wide_half = ((ROWS, LOCAL * HS), F32), ((ROWS, LOCAL * HS), BF16)
    payload = ((RING * (CHUNK + 1), HS), F32)
    sums = ((PEERS * 2 * LINES, HS), F32)
    half_stage = pltpu.VMEM(*wide_half)
    two = [half_stage, half_stage, pltpu.SemaphoreType.DMA((2, TILES))]

    seg_stage, seg_sem = pltpu.VMEM((8, HS), jnp.int32), pltpu.SemaphoreType.DMA
    (tail,) = call(
        tail_kernel, "tail", [payload], (seg, k, v), scratch=[seg_stage, *two, seg_sem], stage=False
    )
    tails = exchange(tail)
    gains = ((LOCAL, HS), F32)
    local, q_open, gains = call(
        local_kernel, "local", [wide, wide_half, gains], (q, k, v, seg, row), (gain,), [SMEM]
    )
    tails, local, q_open, gains = lax.optimization_barrier((tails, local, q_open, gains))
    carry = ((CHUNK + 8, HS), F32)
    row_end, marks = call(row_end_kernel, "row_end", [carry, ((RING, HS), F32)], near=(tails,))
    (before,) = call(before_kernel, "before", [states], near=(tails, marks))
    (before,) = call(carried_over(0), "carry_on", [states], near=(before, marks, to_row(row_end, 1)))
    state_in = exchange(before)
    scaled, part = call(
        attend_kernel,
        "attend",
        [wide, sums],
        (g,),
        (local, q_open, state_in, gains),
        scratch=[half_stage, pltpu.SemaphoreType.DMA((TILES,))],
        stage=False,
    )
    total = over_heads(part)
    inner, back_tail = call(
        inner_kernel, "inner", [wide_half, states], (), (scaled, g, q_open, total, gains)
    )
    back_tails = exchange(back_tail)
    (attended,) = call(attended_kernel, "attended", [wide_half], near=(scaled, total))
    near_v, k_close = call(near_values_kernel, "near_values", [wide, wide_half], (q, k, seg, row), (inner,), out_far=1)
    grad_q, near_k, v_close = call(
        near_queries_kernel, "near_queries", [wide_half, wide, wide_half], (q, k, v, seg, row), (inner, state_in)
    )
    (row_start,) = call(row_start_kernel, "row_start", [carry], near=(back_tails, marks))
    (after,) = call(after_kernel, "after", [states], near=(back_tails, marks))
    (after,) = call(carried_over(1), "carry_back", [states], near=(after, marks, to_row(row_start, -1)))
    state_grad = exchange(after)
    grad_k, grad_v = call(
        far_kernel,
        "far",
        [wide_half, wide_half],
        (k_close,),
        (v_close, near_k, near_v, state_grad),
        out_far=2,
        scratch=[half_stage, *two, pltpu.SemaphoreType.DMA],
        stage=False,
    )
    return attended, grad_q, grad_k, grad_v


def solution(mesh):
    both = P("ctx", "head")
    return jax.shard_map(
        per_device,
        mesh=mesh,
        in_specs=(both, both, both, both, P("ctx"), P("head")),
        out_specs=(both, both, both, both),
        check_vma=False,
    )
```

```python
import jax
import jax.numpy as jnp
from jax import lax
from jax.experimental import pallas as pl
from jax.experimental.pallas import tpu as pltpu
from jax.sharding import PartitionSpec as P

HEADS = 16
HS = 128
EPS = 1e-05

ROWS = 1024
LOCAL = 2
RING = 16
N_ROWS = 4
STEP = 256
WIDE_STEP = 512
TILES = ROWS // STEP
CHUNK = LOCAL * HS // RING

PEERS = 8
LINES = ROWS // HS

VMEM = pl.BlockSpec(memory_space=pltpu.VMEM)
SMEM = pl.BlockSpec(memory_space=pltpu.SMEM)
HBM = pl.BlockSpec(memory_space=pltpu.HBM)
F32 = jnp.float32
BF16 = jnp.bfloat16


def dot(a, b, over):
    return lax.dot_general(
        a, b, (((over[0],), (over[1],)), ((), ())), preferred_element_type=F32
    )


def thirds(x):
    high = x.astype(BF16)
    rest = x - high.astype(F32)
    middle = rest.astype(BF16)
    return [high, middle, (rest - middle.astype(F32)).astype(BF16)]


def together(pairs, sems):
    copies = [pltpu.make_async_copy(a, b, sems.at[i]) for i, (a, b) in enumerate(pairs)]
    for copy in copies:
        copy.start()
    for copy in copies:
        copy.wait()


def staged(kernel, n_in, n_mid, n_out):
    def run(*refs):
        given, rest = refs[:n_in], list(refs[n_in:])
        sems = rest.pop()
        given_held, out_held = rest[n_mid + n_out :][:n_in], rest[n_mid + n_out :][n_in:]
        middle, out = rest[:n_mid], rest[n_mid : n_mid + n_out]
        together(zip(given, given_held), sems)
        kernel(*given_held, *middle, *out_held)
        together(zip(out_held, out), sems)

    return run


def call(kernel, name, outs, far=(), near=(), specs=None, out_far=0, scratch=(), stage=True):
    far = [pltpu.with_memory_space_constraint(x, pltpu.HBM) for x in far]
    if stage and (far or out_far):
        held_outs = outs[len(outs) - out_far :]
        kernel = staged(kernel, len(far), len(near) + len(outs) - out_far, out_far)
        scratch = [pltpu.VMEM(x.shape, x.dtype) for x in far]
        scratch += [pltpu.VMEM(*held) for held in held_outs]
        scratch += [pltpu.SemaphoreType.DMA((len(far) + out_far,))]
    return pl.pallas_call(
        kernel,
        name=name,
        out_shape=[jax.ShapeDtypeStruct(shape, dtype) for shape, dtype in outs],
        in_specs=[HBM] * len(far) + (specs or [VMEM] * len(near)),
        out_specs=[VMEM] * (len(outs) - out_far) + [HBM] * out_far,
        scratch_shapes=list(scratch),
        compiler_params=pltpu.CompilerParams(vmem_limit_bytes=16 << 20),
    )(*far, *near)


def marks_of(seg_ref):
    seg = seg_ref[...].astype(F32)
    opening, closing = jnp.min(seg), jnp.max(seg)
    n_open = jnp.sum(jnp.where(seg == opening, 1.0, 0.0)).astype(jnp.int32)
    n_close = jnp.sum(jnp.where(seg == closing, 1.0, 0.0)).astype(jnp.int32)
    return opening, closing, n_open, ROWS - n_close


def head_of(ref, h, start=0, size=ROWS):
    return ref[start : start + size, h * HS : (h + 1) * HS]


def positions(start, size):
    return start + lax.broadcasted_iota(jnp.int32, (size, HS), 0)


def put_state(out_ref, states, stride):
    flat = jnp.concatenate(states, axis=0)
    for r in range(CHUNK):
        out_ref[pl.ds(r, RING, stride=stride), :] = flat[r * RING : (r + 1) * RING]


def get_state(ref):
    flat = jnp.concatenate([ref[pl.ds(r, RING, stride=CHUNK), :] for r in range(CHUNK)], axis=0)
    return [flat[h * HS : (h + 1) * HS].astype(BF16) for h in range(LOCAL)]


TAIL_TILES = 2
TAIL_STEP = ROWS // TAIL_TILES


def tail_kernel(seg_hbm, k_hbm, v_hbm, out_ref, seg_ref, k_ref, v_ref, sems, seg_sem):
    def copies(i):
        rows = pl.ds(i * TAIL_STEP, TAIL_STEP)
        return [
            pltpu.make_async_copy(k_hbm.at[rows], k_ref.at[rows], sems.at[0, i]),
            pltpu.make_async_copy(v_hbm.at[rows], v_ref.at[rows], sems.at[1, i]),
        ]

    seg_copy = pltpu.make_async_copy(seg_hbm, seg_ref, seg_sem)
    seg_copy.start()
    for i in range(TAIL_TILES):
        for copy in copies(i):
            copy.start()
    seg_copy.wait()
    opening, closing, _, start = marks_of(seg_ref)
    lane = lax.broadcasted_iota(jnp.int32, (RING, HS), 1)
    out_ref[pl.ds(CHUNK, RING, stride=CHUNK + 1), :] = jnp.where(lane == 0, opening, closing) + 1.0
    tails = [jnp.zeros((HS, HS), F32) for _ in range(LOCAL)]
    for i in range(TAIL_TILES):
        for copy in copies(i):
            copy.wait()
        at_close = positions(i * TAIL_STEP, TAIL_STEP) >= start
        for h in range(LOCAL):
            keys = head_of(k_ref, h, i * TAIL_STEP, TAIL_STEP).astype(F32)
            keys = jnp.where(at_close, keys, 0.0).astype(BF16)
            tails[h] = tails[h] + dot(keys, head_of(v_ref, h, i * TAIL_STEP, TAIL_STEP), (0, 0))
    put_state(out_ref, tails, CHUNK + 1)


def chunks_of(x_ref, stride):
    return jnp.concatenate([x_ref[pl.ds(r, RING, stride=stride), :] for r in range(CHUNK)], axis=1)


def summed(chosen, x, out_ref, stride):
    chosen = jnp.where(chosen, 1.0, 0.0).astype(BF16)
    y = dot(jnp.concatenate([chosen] * 3, axis=1), jnp.concatenate(thirds(x), axis=0), (1, 0))
    for r in range(CHUNK):
        own = y[:, r * HS : (r + 1) * HS]
        if stride:
            out_ref[pl.ds(r, RING, stride=stride), :] = own
        else:
            out_ref[r : r + 1, :] = own[0:1]


def iotas(down, along):
    return [lax.broadcasted_iota(jnp.int32, (down, along), d) for d in range(2)]


def as_row(column):
    n = column.shape[0]
    down, along = iotas(n, n)
    return jnp.sum(jnp.where(down == along, column, 0.0), axis=0, keepdims=True)


def row_end_kernel(x_ref, out_ref, marks_ref):
    marks = x_ref[pl.ds(CHUNK, RING, stride=CHUNK + 1), :]
    marks_ref[...] = marks
    closing = marks[RING - 1 : RING, 1:2]
    chosen = jnp.broadcast_to(as_row(marks[:, 1:2]) == closing, (8, RING))
    summed(chosen, chunks_of(x_ref, CHUNK + 1), out_ref, 0)
    out_ref[CHUNK:, :] = jnp.broadcast_to(closing, (8, HS))


def row_start_kernel(x_ref, marks_ref, out_ref):
    opening = marks_ref[0:1, 0:1]
    chosen = jnp.broadcast_to(as_row(marks_ref[:, 0:1]) == opening, (8, RING))
    summed(chosen, chunks_of(x_ref, CHUNK), out_ref, 0)
    out_ref[CHUNK:, :] = jnp.broadcast_to(opening, (8, HS))


def before_kernel(x_ref, marks_ref, out_ref):
    down, along = iotas(RING, RING)
    chosen = (as_row(marks_ref[:, 1:2]) == marks_ref[:, 0:1]) & (along < down)
    summed(chosen, chunks_of(x_ref, CHUNK + 1), out_ref, CHUNK)


def after_kernel(x_ref, marks_ref, out_ref):
    down, along = iotas(RING, RING)
    chosen = (as_row(marks_ref[:, 0:1]) == marks_ref[:, 1:2]) & (along > down)
    summed(chosen, chunks_of(x_ref, CHUNK), out_ref, CHUNK)


def carried_over(side):
    def kernel(x_ref, marks_ref, more_ref, out_ref):
        more = more_ref[:CHUNK, :]
        mark = more_ref[CHUNK : CHUNK + 1, 0:1]
        for block in range(RING):
            joined = marks_ref[block : block + 1, side : side + 1] == mark
            rows = slice(block * CHUNK, (block + 1) * CHUNK)
            out_ref[rows, :] = x_ref[rows, :] + jnp.where(joined, more, 0.0)

    return kernel


def column_of(row):
    return jnp.transpose(jnp.broadcast_to(row, (HS, row.shape[1])))


def allowed_tile(seg_ref, i):
    reach = (i + 1) * STEP
    own = column_of(seg_ref[:, i * STEP : reach].astype(F32))
    same = jnp.concatenate([own] * (reach // HS), axis=1) == seg_ref[:, :reach].astype(F32)
    at = i * STEP + lax.broadcasted_iota(jnp.int32, (STEP, reach), 0)
    return same & (lax.broadcasted_iota(jnp.int32, (STEP, reach), 1) <= at)


def local_kernel(q_ref, k_ref, v_ref, seg_ref, row_ref, gain_ref, out_ref, open_ref, gains_ref):
    _, _, n_open, _ = marks_of(seg_ref)
    for h in range(LOCAL):
        gains_ref[h : h + 1, :] = jnp.full((1, HS), gain_ref[h], F32)
    for i in range(TILES):
        at, reach = i * STEP, (i + 1) * STEP
        allowed = allowed_tile(row_ref, i)
        at_open = positions(at, STEP) < n_open
        for h in range(LOCAL):
            cols = slice(h * HS, (h + 1) * HS)
            query = q_ref[at:reach, cols]
            scores = dot(query, head_of(k_ref, h, 0, reach), (1, 1))
            probs = jnp.where(allowed, scores, 0.0).astype(BF16)
            out_ref[at:reach, cols] = dot(probs, head_of(v_ref, h, 0, reach), (1, 0))
            open_ref[at:reach, cols] = jnp.where(at_open, query.astype(F32), 0.0).astype(BF16)


def line_of(x):
    return jnp.sum(jnp.transpose(x), axis=0, keepdims=True)


def attend_kernel(g_hbm, local_ref, open_ref, state_ref, gain_ref, scaled_ref, sums_ref, g_ref, sems):
    def copy(i):
        rows = pl.ds(i * WIDE_STEP, WIDE_STEP)
        return pltpu.make_async_copy(g_hbm.at[rows], g_ref.at[rows], sems.at[i])

    for i in range((ROWS // WIDE_STEP)):
        copy(i).start()
    states = get_state(state_ref)

    lines = [[], []]

    def put(n, i, x):
        line = line_of(x)
        lines[n] += [line[:, j * HS : (j + 1) * HS] for j in range(WIDE_STEP // HS)]

    for i in range((ROWS // WIDE_STEP)):
        at, reach = i * WIDE_STEP, (i + 1) * WIDE_STEP
        power = jnp.zeros((WIDE_STEP, HS), F32)
        for h in range(LOCAL):
            carried = dot(head_of(open_ref, h, at, WIDE_STEP), states[h], (1, 0))
            scaled = (head_of(local_ref, h, at, WIDE_STEP) + carried) * gain_ref[h : h + 1, :]
            scaled_ref[at:reach, h * HS : (h + 1) * HS] = scaled
            power = power + scaled * scaled
        put(0, i, power)
    for i in range((ROWS // WIDE_STEP)):
        copy(i).wait()
        cross = jnp.zeros((WIDE_STEP, HS), F32)
        for h in range(LOCAL):
            cross = cross + head_of(scaled_ref, h, i * WIDE_STEP, WIDE_STEP) * head_of(g_ref, h, i * WIDE_STEP, WIDE_STEP).astype(F32)
        put(1, i, cross)
    total = jnp.concatenate(lines[0] + lines[1], axis=0)
    for peer in range(PEERS):
        sums_ref[peer * 2 * LINES : (peer + 1) * 2 * LINES, :] = total


def scale_and_pull(sums_ref):
    lines = 2 * LINES
    total = sums_ref[0:lines]
    for peer in range(1, PEERS):
        total = total + sums_ref[peer * lines : (peer + 1) * lines]
    width = HEADS * HS
    scale = lax.rsqrt(total[:LINES] / width + EPS)
    return scale, total[LINES:] * scale * scale * scale / width


def columns_of(lines, i):
    per = STEP // HS
    return jnp.concatenate([column_of(lines[i * per + j : i * per + j + 1]) for j in range(per)], axis=0)


def inner_kernel(scaled_ref, g_ref, open_ref, sums_ref, gain_ref, inner_ref, tail_ref):
    scale, pull = scale_and_pull(sums_ref)
    tails = [jnp.zeros((HS, HS), F32) for _ in range(LOCAL)]
    for i in range(TILES):
        at, reach = i * STEP, (i + 1) * STEP
        scales, pulls = columns_of(scale, i), columns_of(pull, i)
        for h in range(LOCAL):
            cols = slice(h * HS, (h + 1) * HS)
            grad = g_ref[at:reach, cols].astype(F32)
            inner = (gain_ref[h : h + 1, :] * (grad * scales - scaled_ref[at:reach, cols] * pulls)).astype(BF16)
            inner_ref[at:reach, cols] = inner
            tails[h] = tails[h] + dot(open_ref[at:reach, cols], inner, (0, 0))
    put_state(tail_ref, tails, CHUNK)


def attended_kernel(scaled_ref, sums_ref, out_ref):
    scale, _ = scale_and_pull(sums_ref)
    for i in range(TILES):
        at, reach = i * STEP, (i + 1) * STEP
        scales = columns_of(scale, i)
        for h in range(LOCAL):
            cols = slice(h * HS, (h + 1) * HS)
            out_ref[at:reach, cols] = (scaled_ref[at:reach, cols] * scales).astype(BF16)


def at_close_only(ref, start, out_ref):
    for h in range(LOCAL):
        x = jnp.where(positions(0, ROWS) >= start, head_of(ref, h).astype(F32), 0.0)
        out_ref[:, h * HS : (h + 1) * HS] = x.astype(BF16)


def near_queries_kernel(
    q_ref, k_ref, v_ref, seg_ref, row_ref, inner_ref, state_ref, gq_ref, keys_ref, closing_ref, again_ref
):
    again_ref[...] = inner_ref[...]
    _, _, n_open, start = marks_of(seg_ref)
    at_close_only(v_ref, start, closing_ref)
    states = get_state(state_ref)
    keys_ref[...] = jnp.zeros(keys_ref.shape, F32)
    for i in range(TILES):
        at, reach = i * STEP, (i + 1) * STEP
        allowed = allowed_tile(row_ref, i)
        at_open = positions(at, STEP) < n_open
        for h in range(LOCAL):
            cols = slice(h * HS, (h + 1) * HS)
            inner = inner_ref[at:reach, cols]
            dscores = dot(inner, v_ref[:reach, cols], (1, 1))
            dprobs = jnp.where(allowed, dscores, 0.0).astype(BF16)
            grad_q = dot(dprobs, k_ref[:reach, cols], (1, 0))
            grad_q = grad_q + jnp.where(at_open, dot(inner, states[h], (1, 1)), 0.0)
            gq_ref[at:reach, cols] = grad_q.astype(BF16)
            keys_ref[:reach, cols] += dot(dprobs, q_ref[at:reach, cols], (0, 0))


def near_values_kernel(q_ref, k_ref, seg_ref, row_ref, inner_ref, values_ref, closing_ref):
    _, _, _, start = marks_of(seg_ref)
    at_close_only(k_ref, start, closing_ref)
    values_ref[...] = jnp.zeros(values_ref.shape, F32)
    for i in range(TILES):
        at, reach = i * STEP, (i + 1) * STEP
        allowed = allowed_tile(row_ref, i)
        for h in range(LOCAL):
            cols = slice(h * HS, (h + 1) * HS)
            scores = dot(q_ref[at:reach, cols], k_ref[:reach, cols], (1, 1))
            probs = jnp.where(allowed, scores, 0.0).astype(BF16)
            values_ref[:reach, cols] += dot(probs, inner_ref[at:reach, cols], (0, 0))


def far_kernel(
    k_ref, v_ref, keys_ref, values_ref, back_ref, gk_hbm, gv_hbm, gk_ref, gv_ref, sems
):
    backs = get_state(back_ref)
    copies = []
    for i in range(ROWS // WIDE_STEP):
        at, reach = i * WIDE_STEP, (i + 1) * WIDE_STEP
        rows = pl.ds(at, WIDE_STEP)
        for h in range(LOCAL):
            cols = slice(h * HS, (h + 1) * HS)
            far = dot(v_ref[at:reach, cols], backs[h], (1, 1))
            gk_ref[at:reach, cols] = (keys_ref[at:reach, cols] + far).astype(BF16)
        copies.append(pltpu.make_async_copy(gk_ref.at[rows], gk_hbm.at[rows], sems.at[0, i]))
        copies[-1].start()
    for i in range(ROWS // WIDE_STEP):
        at, reach = i * WIDE_STEP, (i + 1) * WIDE_STEP
        rows = pl.ds(at, WIDE_STEP)
        for h in range(LOCAL):
            cols = slice(h * HS, (h + 1) * HS)
            far = dot(k_ref[at:reach, cols], backs[h], (1, 0))
            gv_ref[at:reach, cols] = (values_ref[at:reach, cols] + far).astype(BF16)
        copies.append(pltpu.make_async_copy(gv_ref.at[rows], gv_hbm.at[rows], sems.at[1, i]))
        copies[-1].start()
    for copy in copies:
        copy.wait()


def exchange(x):
    parts = x.reshape(RING, 1, -1)
    rings = [[y * RING + z for z in range(RING)] for y in range(N_ROWS)]
    out = lax.all_to_all(parts, "ctx", 0, 0, axis_index_groups=rings, tiled=True)
    return out.reshape(x.shape)


def to_row(x, by):
    pairs = [(i, i + by * RING) for i in range(N_ROWS * RING)]
    return lax.ppermute(x, "ctx", [(a, b) for a, b in pairs if 0 <= b < N_ROWS * RING])


def over_heads(x):
    parts = x.reshape(PEERS, 1, -1)
    return lax.all_to_all(parts, "head", 0, 0, tiled=True).reshape(x.shape)


def per_device(queries, key_vectors, value_vectors, out_grad, segment_ids, head_gain):
    q, k, v, g, gain = queries, key_vectors, value_vectors, out_grad, head_gain
    seg = segment_ids.reshape(8, HS)
    row = segment_ids.reshape(1, ROWS)
    states = ((RING * CHUNK, HS), F32)
    wide, wide_half = ((ROWS, LOCAL * HS), F32), ((ROWS, LOCAL * HS), BF16)
    payload = ((RING * (CHUNK + 1), HS), F32)
    sums = ((PEERS * 2 * LINES, HS), F32)
    half_stage = pltpu.VMEM(*wide_half)
    two = [half_stage, half_stage, pltpu.SemaphoreType.DMA((2, TILES))]

    seg_stage, seg_sem = pltpu.VMEM((8, HS), jnp.int32), pltpu.SemaphoreType.DMA
    (tail,) = call(
        tail_kernel, "tail", [payload], (seg, k, v), scratch=[seg_stage, *two, seg_sem], stage=False
    )
    tails = exchange(tail)
    gains = ((LOCAL, HS), F32)
    local, q_open, gains = call(
        local_kernel, "local", [wide, wide_half, gains], (q, k, v, seg, row), (gain,), [SMEM]
    )
    tails, local, q_open, gains = lax.optimization_barrier((tails, local, q_open, gains))
    carry = ((CHUNK + 8, HS), F32)
    row_end, marks = call(row_end_kernel, "row_end", [carry, ((RING, HS), F32)], near=(tails,))
    (before,) = call(before_kernel, "before", [states], near=(tails, marks))
    (before,) = call(carried_over(0), "carry_on", [states], near=(before, marks, to_row(row_end, 1)))
    state_in = exchange(before)
    scaled, part = call(
        attend_kernel,
        "attend",
        [wide, sums],
        (g,),
        (local, q_open, state_in, gains),
        scratch=[half_stage, pltpu.SemaphoreType.DMA((TILES,))],
        stage=False,
    )
    total = over_heads(part)
    inner, back_tail = call(
        inner_kernel, "inner", [wide_half, states], (), (scaled, g, q_open, total, gains)
    )
    back_tails = exchange(back_tail)
    (attended,) = call(attended_kernel, "attended", [wide_half], near=(scaled, total))
    grad_q, near_k, v_close, again = call(
        near_queries_kernel,
        "near_queries",
        [wide_half, wide, wide_half, wide_half],
        (q, k, v, seg, row),
        (inner, state_in),
    )
    near_v, k_close = call(near_values_kernel, "near_values", [wide, wide_half], (q, k, seg, row), (again,))
    (row_start,) = call(row_start_kernel, "row_start", [carry], near=(back_tails, marks))
    (after,) = call(after_kernel, "after", [states], near=(back_tails, marks))
    (after,) = call(carried_over(1), "carry_back", [states], near=(after, marks, to_row(row_start, -1)))
    state_grad = exchange(after)
    grad_k, grad_v = call(
        far_kernel,
        "far",
        [wide_half, wide_half],
        near=(k_close, v_close, near_k, near_v, state_grad),
        out_far=2,
        scratch=two,
        stage=False,
    )
    return attended, grad_q, grad_k, grad_v


def solution(mesh):
    both = P("ctx", "head")
    return jax.shard_map(
        per_device,
        mesh=mesh,
        in_specs=(both, both, both, both, P("ctx"), P("head")),
        out_specs=(both, both, both, both),
        check_vma=False,
    )
```

```python
import jax
import jax.numpy as jnp
from jax import lax
from jax.experimental import pallas as pl
from jax.experimental.pallas import tpu as pltpu
from jax.sharding import PartitionSpec as P

HEADS = 16
HS = 128
EPS = 1e-05

ROWS = 1024
LOCAL = 2
RING = 16
N_ROWS = 4
STEP = 256
WIDE_STEP = 512
TILES = ROWS // STEP
CHUNK = LOCAL * HS // RING

PEERS = 8
LINES = ROWS // HS

VMEM = pl.BlockSpec(memory_space=pltpu.VMEM)
SMEM = pl.BlockSpec(memory_space=pltpu.SMEM)
HBM = pl.BlockSpec(memory_space=pltpu.HBM)
F32 = jnp.float32
BF16 = jnp.bfloat16


def dot(a, b, over):
    return lax.dot_general(
        a, b, (((over[0],), (over[1],)), ((), ())), preferred_element_type=F32
    )


def thirds(x):
    high = x.astype(BF16)
    rest = x - high.astype(F32)
    middle = rest.astype(BF16)
    return [high, middle, (rest - middle.astype(F32)).astype(BF16)]


def together(pairs, sems):
    copies = [pltpu.make_async_copy(a, b, sems.at[i]) for i, (a, b) in enumerate(pairs)]
    for copy in copies:
        copy.start()
    for copy in copies:
        copy.wait()


def staged(kernel, n_in, n_mid, n_out):
    def run(*refs):
        given, rest = refs[:n_in], list(refs[n_in:])
        sems = rest.pop()
        given_held, out_held = rest[n_mid + n_out :][:n_in], rest[n_mid + n_out :][n_in:]
        middle, out = rest[:n_mid], rest[n_mid : n_mid + n_out]
        together(zip(given, given_held), sems)
        kernel(*given_held, *middle, *out_held)
        together(zip(out_held, out), sems)

    return run


def call(kernel, name, outs, far=(), near=(), specs=None, out_far=0, scratch=(), stage=True):
    far = [pltpu.with_memory_space_constraint(x, pltpu.HBM) for x in far]
    if stage and (far or out_far):
        held_outs = outs[len(outs) - out_far :]
        kernel = staged(kernel, len(far), len(near) + len(outs) - out_far, out_far)
        scratch = [pltpu.VMEM(x.shape, x.dtype) for x in far]
        scratch += [pltpu.VMEM(*held) for held in held_outs]
        scratch += [pltpu.SemaphoreType.DMA((len(far) + out_far,))]
    return pl.pallas_call(
        kernel,
        name=name,
        out_shape=[jax.ShapeDtypeStruct(shape, dtype) for shape, dtype in outs],
        in_specs=[HBM] * len(far) + (specs or [VMEM] * len(near)),
        out_specs=[VMEM] * (len(outs) - out_far) + [HBM] * out_far,
        scratch_shapes=list(scratch),
        compiler_params=pltpu.CompilerParams(vmem_limit_bytes=16 << 20),
    )(*far, *near)


def marks_of(seg_ref):
    seg = seg_ref[...].astype(F32)
    opening, closing = jnp.min(seg), jnp.max(seg)
    n_open = jnp.sum(jnp.where(seg == opening, 1.0, 0.0)).astype(jnp.int32)
    n_close = jnp.sum(jnp.where(seg == closing, 1.0, 0.0)).astype(jnp.int32)
    return opening, closing, n_open, ROWS - n_close


def head_of(ref, h, start=0, size=ROWS):
    return ref[start : start + size, h * HS : (h + 1) * HS]


def positions(start, size):
    return start + lax.broadcasted_iota(jnp.int32, (size, HS), 0)


def put_state(out_ref, states, stride):
    flat = jnp.concatenate(states, axis=0)
    for r in range(CHUNK):
        out_ref[pl.ds(r, RING, stride=stride), :] = flat[r * RING : (r + 1) * RING]


def get_state(ref):
    flat = jnp.concatenate([ref[pl.ds(r, RING, stride=CHUNK), :] for r in range(CHUNK)], axis=0)
    return [flat[h * HS : (h + 1) * HS].astype(BF16) for h in range(LOCAL)]


TAIL_TILES = 1
TAIL_STEP = ROWS // TAIL_TILES


def tail_kernel(seg_hbm, k_hbm, v_hbm, out_ref, seg_ref, k_ref, v_ref, sems, seg_sem):
    def copies(i):
        rows = pl.ds(i * TAIL_STEP, TAIL_STEP)
        return [
            pltpu.make_async_copy(k_hbm.at[rows], k_ref.at[rows], sems.at[0, i]),
            pltpu.make_async_copy(v_hbm.at[rows], v_ref.at[rows], sems.at[1, i]),
        ]

    seg_copy = pltpu.make_async_copy(seg_hbm, seg_ref, seg_sem)
    seg_copy.start()
    for i in range(TAIL_TILES):
        for copy in copies(i):
            copy.start()
    seg_copy.wait()
    opening, closing, _, start = marks_of(seg_ref)
    lane = lax.broadcasted_iota(jnp.int32, (RING, HS), 1)
    out_ref[pl.ds(CHUNK, RING, stride=CHUNK + 1), :] = jnp.where(lane == 0, opening, closing) + 1.0
    tails = [jnp.zeros((HS, HS), F32) for _ in range(LOCAL)]
    for i in range(TAIL_TILES):
        for copy in copies(i):
            copy.wait()
        at_close = positions(i * TAIL_STEP, TAIL_STEP) >= start
        for h in range(LOCAL):
            keys = head_of(k_ref, h, i * TAIL_STEP, TAIL_STEP).astype(F32)
            keys = jnp.where(at_close, keys, 0.0).astype(BF16)
            tails[h] = tails[h] + dot(keys, head_of(v_ref, h, i * TAIL_STEP, TAIL_STEP), (0, 0))
    put_state(out_ref, tails, CHUNK + 1)


def chunks_of(x_ref, stride):
    return jnp.concatenate([x_ref[pl.ds(r, RING, stride=stride), :] for r in range(CHUNK)], axis=1)


def summed(chosen, x, out_ref, stride):
    chosen = jnp.where(chosen, 1.0, 0.0).astype(BF16)
    y = dot(jnp.concatenate([chosen] * 3, axis=1), jnp.concatenate(thirds(x), axis=0), (1, 0))
    for r in range(CHUNK):
        own = y[:, r * HS : (r + 1) * HS]
        if stride:
            out_ref[pl.ds(r, RING, stride=stride), :] = own
        else:
            out_ref[r : r + 1, :] = own[0:1]


def iotas(down, along):
    return [lax.broadcasted_iota(jnp.int32, (down, along), d) for d in range(2)]


def as_row(column):
    n = column.shape[0]
    down, along = iotas(n, n)
    return jnp.sum(jnp.where(down == along, column, 0.0), axis=0, keepdims=True)


def row_end_kernel(x_ref, out_ref, marks_ref):
    marks = x_ref[pl.ds(CHUNK, RING, stride=CHUNK + 1), :]
    marks_ref[...] = marks
    closing = marks[RING - 1 : RING, 1:2]
    chosen = jnp.broadcast_to(as_row(marks[:, 1:2]) == closing, (8, RING))
    summed(chosen, chunks_of(x_ref, CHUNK + 1), out_ref, 0)
    out_ref[CHUNK:, :] = jnp.broadcast_to(closing, (8, HS))


def row_start_kernel(x_ref, marks_ref, out_ref):
    opening = marks_ref[0:1, 0:1]
    chosen = jnp.broadcast_to(as_row(marks_ref[:, 0:1]) == opening, (8, RING))
    summed(chosen, chunks_of(x_ref, CHUNK), out_ref, 0)
    out_ref[CHUNK:, :] = jnp.broadcast_to(opening, (8, HS))


def before_kernel(x_ref, marks_ref, out_ref):
    down, along = iotas(RING, RING)
    chosen = (as_row(marks_ref[:, 1:2]) == marks_ref[:, 0:1]) & (along < down)
    summed(chosen, chunks_of(x_ref, CHUNK + 1), out_ref, CHUNK)


def after_kernel(x_ref, marks_ref, out_ref):
    down, along = iotas(RING, RING)
    chosen = (as_row(marks_ref[:, 0:1]) == marks_ref[:, 1:2]) & (along > down)
    summed(chosen, chunks_of(x_ref, CHUNK), out_ref, CHUNK)


def carried_over(side):
    def kernel(x_ref, marks_ref, more_ref, out_ref):
        more = more_ref[:CHUNK, :]
        mark = more_ref[CHUNK : CHUNK + 1, 0:1]
        for block in range(RING):
            joined = marks_ref[block : block + 1, side : side + 1] == mark
            rows = slice(block * CHUNK, (block + 1) * CHUNK)
            out_ref[rows, :] = x_ref[rows, :] + jnp.where(joined, more, 0.0)

    return kernel


def column_of(row):
    return jnp.transpose(jnp.broadcast_to(row, (HS, row.shape[1])))


def allowed_tile(seg_ref, i):
    reach = (i + 1) * STEP
    own = column_of(seg_ref[:, i * STEP : reach].astype(F32))
    same = jnp.concatenate([own] * (reach // HS), axis=1) == seg_ref[:, :reach].astype(F32)
    at = i * STEP + lax.broadcasted_iota(jnp.int32, (STEP, reach), 0)
    return same & (lax.broadcasted_iota(jnp.int32, (STEP, reach), 1) <= at)


def local_kernel(q_ref, k_ref, v_ref, seg_ref, row_ref, gain_ref, out_ref, open_ref, gains_ref):
    _, _, n_open, _ = marks_of(seg_ref)
    for h in range(LOCAL):
        gains_ref[h : h + 1, :] = jnp.full((1, HS), gain_ref[h], F32)
    for i in range(TILES):
        at, reach = i * STEP, (i + 1) * STEP
        allowed = allowed_tile(row_ref, i)
        at_open = positions(at, STEP) < n_open
        for h in range(LOCAL):
            cols = slice(h * HS, (h + 1) * HS)
            query = q_ref[at:reach, cols]
            scores = dot(query, head_of(k_ref, h, 0, reach), (1, 1))
            probs = jnp.where(allowed, scores, 0.0).astype(BF16)
            out_ref[at:reach, cols] = dot(probs, head_of(v_ref, h, 0, reach), (1, 0))
            open_ref[at:reach, cols] = jnp.where(at_open, query.astype(F32), 0.0).astype(BF16)


def line_of(x):
    return jnp.sum(jnp.transpose(x), axis=0, keepdims=True)


def attend_kernel(g_hbm, local_ref, open_ref, state_ref, gain_ref, scaled_ref, sums_ref, g_ref, sems):
    def copy(i):
        rows = pl.ds(i * WIDE_STEP, WIDE_STEP)
        return pltpu.make_async_copy(g_hbm.at[rows], g_ref.at[rows], sems.at[i])

    for i in range((ROWS // WIDE_STEP)):
        copy(i).start()
    states = get_state(state_ref)

    lines = [[], []]

    def put(n, i, x):
        line = line_of(x)
        lines[n] += [line[:, j * HS : (j + 1) * HS] for j in range(WIDE_STEP // HS)]

    for i in range((ROWS // WIDE_STEP)):
        at, reach = i * WIDE_STEP, (i + 1) * WIDE_STEP
        power = jnp.zeros((WIDE_STEP, HS), F32)
        for h in range(LOCAL):
            carried = dot(head_of(open_ref, h, at, WIDE_STEP), states[h], (1, 0))
            scaled = (head_of(local_ref, h, at, WIDE_STEP) + carried) * gain_ref[h : h + 1, :]
            scaled_ref[at:reach, h * HS : (h + 1) * HS] = scaled
            power = power + scaled * scaled
        put(0, i, power)
    for i in range((ROWS // WIDE_STEP)):
        copy(i).wait()
        cross = jnp.zeros((WIDE_STEP, HS), F32)
        for h in range(LOCAL):
            cross = cross + head_of(scaled_ref, h, i * WIDE_STEP, WIDE_STEP) * head_of(g_ref, h, i * WIDE_STEP, WIDE_STEP).astype(F32)
        put(1, i, cross)
    total = jnp.concatenate(lines[0] + lines[1], axis=0)
    for peer in range(PEERS):
        sums_ref[peer * 2 * LINES : (peer + 1) * 2 * LINES, :] = total


def scale_and_pull(sums_ref):
    lines = 2 * LINES
    total = sums_ref[0:lines]
    for peer in range(1, PEERS):
        total = total + sums_ref[peer * lines : (peer + 1) * lines]
    width = HEADS * HS
    scale = lax.rsqrt(total[:LINES] / width + EPS)
    return scale, total[LINES:] * scale * scale * scale / width


def columns_of(lines, i):
    per = STEP // HS
    return jnp.concatenate([column_of(lines[i * per + j : i * per + j + 1]) for j in range(per)], axis=0)


def inner_kernel(scaled_ref, g_ref, open_ref, sums_ref, gain_ref, inner_ref, tail_ref):
    scale, pull = scale_and_pull(sums_ref)
    tails = [jnp.zeros((HS, HS), F32) for _ in range(LOCAL)]
    for i in range(TILES):
        at, reach = i * STEP, (i + 1) * STEP
        scales, pulls = columns_of(scale, i), columns_of(pull, i)
        for h in range(LOCAL):
            cols = slice(h * HS, (h + 1) * HS)
            grad = g_ref[at:reach, cols].astype(F32)
            inner = (gain_ref[h : h + 1, :] * (grad * scales - scaled_ref[at:reach, cols] * pulls)).astype(BF16)
            inner_ref[at:reach, cols] = inner
            tails[h] = tails[h] + dot(open_ref[at:reach, cols], inner, (0, 0))
    put_state(tail_ref, tails, CHUNK)


def attended_kernel(scaled_ref, sums_ref, out_ref):
    scale, _ = scale_and_pull(sums_ref)
    for i in range(TILES):
        at, reach = i * STEP, (i + 1) * STEP
        scales = columns_of(scale, i)
        for h in range(LOCAL):
            cols = slice(h * HS, (h + 1) * HS)
            out_ref[at:reach, cols] = (scaled_ref[at:reach, cols] * scales).astype(BF16)


def at_close_only(ref, start, out_ref):
    for h in range(LOCAL):
        x = jnp.where(positions(0, ROWS) >= start, head_of(ref, h).astype(F32), 0.0)
        out_ref[:, h * HS : (h + 1) * HS] = x.astype(BF16)


def near_queries_kernel(
    q_ref, k_ref, v_ref, seg_ref, row_ref, inner_ref, state_ref, gq_ref, keys_ref, closing_ref, again_ref
):
    again_ref[...] = inner_ref[...]
    _, _, n_open, start = marks_of(seg_ref)
    at_close_only(v_ref, start, closing_ref)
    states = get_state(state_ref)
    keys_ref[...] = jnp.zeros(keys_ref.shape, F32)
    for i in range(TILES):
        at, reach = i * STEP, (i + 1) * STEP
        allowed = allowed_tile(row_ref, i)
        at_open = positions(at, STEP) < n_open
        for h in range(LOCAL):
            cols = slice(h * HS, (h + 1) * HS)
            inner = inner_ref[at:reach, cols]
            dscores = dot(inner, v_ref[:reach, cols], (1, 1))
            dprobs = jnp.where(allowed, dscores, 0.0).astype(BF16)
            grad_q = dot(dprobs, k_ref[:reach, cols], (1, 0))
            grad_q = grad_q + jnp.where(at_open, dot(inner, states[h], (1, 1)), 0.0)
            gq_ref[at:reach, cols] = grad_q.astype(BF16)
            keys_ref[:reach, cols] += dot(dprobs, q_ref[at:reach, cols], (0, 0))


def near_values_kernel(q_ref, k_ref, seg_ref, row_ref, inner_ref, values_ref, closing_ref):
    _, _, _, start = marks_of(seg_ref)
    at_close_only(k_ref, start, closing_ref)
    values_ref[...] = jnp.zeros(values_ref.shape, F32)
    for i in range(TILES):
        at, reach = i * STEP, (i + 1) * STEP
        allowed = allowed_tile(row_ref, i)
        for h in range(LOCAL):
            cols = slice(h * HS, (h + 1) * HS)
            scores = dot(q_ref[at:reach, cols], k_ref[:reach, cols], (1, 1))
            probs = jnp.where(allowed, scores, 0.0).astype(BF16)
            values_ref[:reach, cols] += dot(probs, inner_ref[at:reach, cols], (0, 0))


def far_kernel(
    k_ref, v_ref, keys_ref, values_ref, back_ref, gk_hbm, gv_hbm, gk_ref, gv_ref, sems
):
    backs = get_state(back_ref)
    copies = []
    for i in range(ROWS // WIDE_STEP):
        at, reach = i * WIDE_STEP, (i + 1) * WIDE_STEP
        rows = pl.ds(at, WIDE_STEP)
        for h in range(LOCAL):
            cols = slice(h * HS, (h + 1) * HS)
            far = dot(v_ref[at:reach, cols], backs[h], (1, 1))
            gk_ref[at:reach, cols] = (keys_ref[at:reach, cols] + far).astype(BF16)
        copies.append(pltpu.make_async_copy(gk_ref.at[rows], gk_hbm.at[rows], sems.at[0, i]))
        copies[-1].start()
    for i in range(ROWS // WIDE_STEP):
        at, reach = i * WIDE_STEP, (i + 1) * WIDE_STEP
        rows = pl.ds(at, WIDE_STEP)
        for h in range(LOCAL):
            cols = slice(h * HS, (h + 1) * HS)
            far = dot(k_ref[at:reach, cols], backs[h], (1, 0))
            gv_ref[at:reach, cols] = (values_ref[at:reach, cols] + far).astype(BF16)
        copies.append(pltpu.make_async_copy(gv_ref.at[rows], gv_hbm.at[rows], sems.at[1, i]))
        copies[-1].start()
    for copy in copies:
        copy.wait()


def exchange(x):
    parts = x.reshape(RING, 1, -1)
    rings = [[y * RING + z for z in range(RING)] for y in range(N_ROWS)]
    out = lax.all_to_all(parts, "ctx", 0, 0, axis_index_groups=rings, tiled=True)
    return out.reshape(x.shape)


def to_row(x, by):
    pairs = [(i, i + by * RING) for i in range(N_ROWS * RING)]
    return lax.ppermute(x, "ctx", [(a, b) for a, b in pairs if 0 <= b < N_ROWS * RING])


def over_heads(x):
    parts = x.reshape(PEERS, 1, -1)
    return lax.all_to_all(parts, "head", 0, 0, tiled=True).reshape(x.shape)


def per_device(queries, key_vectors, value_vectors, out_grad, segment_ids, head_gain):
    q, k, v, g, gain = queries, key_vectors, value_vectors, out_grad, head_gain
    seg = segment_ids.reshape(8, HS)
    row = segment_ids.reshape(1, ROWS)
    states = ((RING * CHUNK, HS), F32)
    wide, wide_half = ((ROWS, LOCAL * HS), F32), ((ROWS, LOCAL * HS), BF16)
    payload = ((RING * (CHUNK + 1), HS), F32)
    sums = ((PEERS * 2 * LINES, HS), F32)
    half_stage = pltpu.VMEM(*wide_half)
    two = [half_stage, half_stage, pltpu.SemaphoreType.DMA((2, TILES))]

    seg_stage, seg_sem = pltpu.VMEM((8, HS), jnp.int32), pltpu.SemaphoreType.DMA
    (tail,) = call(
        tail_kernel, "tail", [payload], (seg, k, v), scratch=[seg_stage, *two, seg_sem], stage=False
    )
    tails = exchange(tail)
    gains = ((LOCAL, HS), F32)
    local, q_open, gains = call(
        local_kernel, "local", [wide, wide_half, gains], (q, k, v, seg, row), (gain,), [SMEM]
    )
    tails, local, q_open, gains = lax.optimization_barrier((tails, local, q_open, gains))
    carry = ((CHUNK + 8, HS), F32)
    row_end, marks = call(row_end_kernel, "row_end", [carry, ((RING, HS), F32)], near=(tails,))
    (before,) = call(before_kernel, "before", [states], near=(tails, marks))
    (before,) = call(carried_over(0), "carry_on", [states], near=(before, marks, to_row(row_end, 1)))
    state_in = exchange(before)
    scaled, part = call(
        attend_kernel,
        "attend",
        [wide, sums],
        (g,),
        (local, q_open, state_in, gains),
        scratch=[half_stage, pltpu.SemaphoreType.DMA((TILES,))],
        stage=False,
    )
    total = over_heads(part)
    inner, back_tail = call(
        inner_kernel, "inner", [wide_half, states], (), (scaled, g, q_open, total, gains)
    )
    back_tails = exchange(back_tail)
    (attended,) = call(attended_kernel, "attended", [wide_half], near=(scaled, total))
    grad_q, near_k, v_close, again = call(
        near_queries_kernel,
        "near_queries",
        [wide_half, wide, wide_half, wide_half],
        (q, k, v, seg, row),
        (inner, state_in),
    )
    near_v, k_close = call(near_values_kernel, "near_values", [wide, wide_half], (q, k, seg, row), (again,))
    (row_start,) = call(row_start_kernel, "row_start", [carry], near=(back_tails, marks))
    (after,) = call(after_kernel, "after", [states], near=(back_tails, marks))
    (after,) = call(carried_over(1), "carry_back", [states], near=(after, marks, to_row(row_start, -1)))
    state_grad = exchange(after)
    grad_k, grad_v = call(
        far_kernel,
        "far",
        [wide_half, wide_half],
        near=(k_close, v_close, near_k, near_v, state_grad),
        out_far=2,
        scratch=two,
        stage=False,
    )
    return attended, grad_q, grad_k, grad_v


def solution(mesh):
    both = P("ctx", "head")
    return jax.shard_map(
        per_device,
        mesh=mesh,
        in_specs=(both, both, both, both, P("ctx"), P("head")),
        out_specs=(both, both, both, both),
        check_vma=False,
    )
```
